256 devices in a mesh: dp: 16 (over x, y), ctx: 16 (over z, core).
Axes of the slice: x: 4, y: 4, z: 8, core: 2. Of those that a mesh axis runs over, the one named last changes fastest.
Arguments:
- queries: bfloat16 [16, 4096, 1024], P('dp', 'ctx'), may hold values from -12 to 12
- keyvals: bfloat16 [16, 4096, 256], P('dp', 'ctx'), may hold values from -6 to 6
- dest_bin: int32 [16, 4096], P('dp', 'ctx'), may hold values from 0 to 15, as said below
- source_owner: int32 [16, 4096], P('dp', 'ctx'), may hold values from 0 to 15, as said below
- seq_lengths: int32 [16, 4], P('dp'), may hold values from 1 to 3072, 4096 in all within a row
Outputs:
- attended: bfloat16 [16, 4096, 1024], P('dp', 'ctx')
The draws below stay inside these ranges and needn't reach their ends.
Inputs may be any that keep to these rules, and one draw needn't show every extreme that they name: In every block c and for every owner o and bin b, the positions of block c of owner o with dest_bin b are as many as the positions of block c of bin b with source_owner o, and at most 32; in every block some owner sends exactly 32 to some bin. `source_owner`: matches dest_bin as stated there.
All inputs are finite; a program needn't handle non-finite values.
Results may differ from the reference program's by a relative error of at most 0.0065.
Values may be sent and summed in bfloat16 or wider, within the bound.
No kernel may reach another device: no remote copies, remote signals or barrier semaphores. Data moves between devices by JAX's collectives and lax.ppermute only.
A program may use at most 128 MiB of HBM per device.

```python
import math
import jax
import jax.numpy as jnp
import numpy as np
from jax import lax

HEAD = 128
QPG = 8
TOK_DEV = 256
SEQ_BIN = 4
TOKENS_BIN = 4096
MOST = 3072
CAP = 32
N_DP = 16
N_CTX = 16


def plan_counts(key):
    spare = TOK_DEV - CAP
    share = spare // (N_DP - 1)
    extra = spare % (N_DP - 1)
    base_key = jax.random.fold_in(key, 11)

    def column(column_no):
        column_key = jax.random.fold_in(base_key, column_no)
        jitter = jax.random.randint(jax.random.fold_in(column_key, 1), (N_DP - 1,), 0, share // 2 + 1)
        others = share + (jnp.arange(N_DP - 1) < extra).astype(jnp.int32) + jitter - jnp.roll(jitter, 1)
        weights = jnp.concatenate([jnp.full((1,), CAP, jnp.int32), others.astype(jnp.int32)])
        weights = jax.random.permutation(jax.random.fold_in(column_key, 2), weights)
        owner = jnp.arange(N_DP)[:, None]
        target = jnp.arange(N_DP)[None, :]
        return weights[(target - owner) % N_DP]
    return jax.vmap(column)(jnp.arange(N_CTX))


def spread_rows(counts, row_key):
    bounds = jnp.cumsum(counts)
    labels = jnp.sum((jnp.arange(TOK_DEV)[:, None] >= bounds[None, :]).astype(jnp.int32), axis=1)
    return jax.random.permutation(row_key, labels).astype(jnp.int32)


def labels_for(key, salt, outgoing):
    counts = plan_counts(key)
    salted = jax.random.fold_in(key, salt)

    def one(column_no, device_no):
        picked = counts[column_no, device_no, :] if outgoing else counts[column_no, :, device_no]
        return spread_rows(picked, jax.random.fold_in(salted, column_no * N_DP + device_no))
    grid = jax.vmap(lambda column_no: jax.vmap(lambda device_no: one(column_no, device_no))(jnp.arange(N_DP)))(jnp.arange(N_CTX))
    return jnp.transpose(grid, (1, 0, 2)).reshape(N_DP, TOKENS_BIN).astype(jnp.int32)


def draw_dest_bin(key, part):
    return labels_for(key, 23, True)


def draw_source_owner(key, part):
    return labels_for(key, 29, False)


def draw_queries(key, part):
    shape = (N_DP, TOKENS_BIN, QPG, HEAD)
    own = jax.random.fold_in(key, 3)
    result = jnp.clip(jax.random.normal(jax.random.fold_in(own, 1), shape, jnp.float32), -6.0, 6.0)
    return result.reshape(N_DP, TOKENS_BIN, QPG * HEAD).astype(jnp.bfloat16)


def draw_keyvals(key, part):
    shape = (N_DP, TOKENS_BIN, HEAD)
    own = jax.random.fold_in(key, 5)
    key_part = jnp.clip(jax.random.normal(jax.random.fold_in(own, 1), shape, jnp.float32), -6.0, 6.0)
    value_part = jnp.clip(jax.random.normal(jax.random.fold_in(own, 2), shape, jnp.float32), -6.0, 6.0)
    return jnp.concatenate([key_part, value_part], axis=-1).astype(jnp.bfloat16)


def split_up(number_of, total, most, slope):
    loads = [(1 << 20) // math.isqrt(grade ** slope) + 1 for grade in range(2, number_of + 1)]
    surplus, given = total - most - (number_of - 1), [1] * (number_of - 1)
    while surplus > 0:
        candidates = [i for i in range(number_of - 1) if given[i] < most]
        pool, left = sum([loads[i] for i in candidates]), surplus
        for i in candidates:
            more = min(most - given[i], max(1, left * loads[i] // pool), surplus)
            given[i] = given[i] + more
            surplus = surplus - more
    return np.array([most] + given)


def ragged(key, number_of, total, limit, lean):
    if number_of == 2:
        one = jax.random.randint(key, (), max(1, total - limit), min(limit, total - 1) + 1)
        return jnp.stack([one, total - one])
    tallies = jnp.asarray(split_up(number_of, total, limit, lean), jnp.int32)
    pairs = (number_of - 1) // 2
    giver, taker = tallies[1:1 + 2 * pairs:2], tallies[2:2 + 2 * pairs:2]
    margin = jnp.minimum(giver - 1, limit - taker)
    passed = jax.random.randint(jax.random.fold_in(key, 1), (pairs,), 0, 1 << 20) % (margin + 1)
    tallies = tallies.at[1:1 + 2 * pairs:2].set(giver - passed).at[2:2 + 2 * pairs:2].set(taker + passed)
    return tallies[jax.random.permutation(jax.random.fold_in(key, 2), number_of)]


def setup_inputs(seed: int = 0) -> dict:
    arg_keys = jax.random.split(jax.random.key(seed), 6)
    return {
        "queries": draw_queries(jax.random.fold_in(arg_keys[5], 71), 0),
        "keyvals": draw_keyvals(jax.random.fold_in(arg_keys[5], 71), 0),
        "dest_bin": draw_dest_bin(jax.random.fold_in(arg_keys[5], 71), 0),
        "source_owner": draw_source_owner(jax.random.fold_in(arg_keys[5], 71), 0),
        "seq_lengths": jax.vmap(lambda own: ragged(own, SEQ_BIN, TOKENS_BIN, MOST, 2))(jax.random.split(arg_keys[4], N_DP)).reshape((N_DP, SEQ_BIN)).astype(jnp.int32),
    }


def rank_within(labels):
    onehot = (labels[..., None] == jnp.arange(N_DP, dtype=jnp.int32)).astype(jnp.int32)
    running = jnp.cumsum(onehot, axis=-2) - 1
    return jnp.sum(running * onehot, axis=-1).astype(jnp.int32)


def attend_bin(operands):
    bin_q, bin_kv, lengths = operands
    seg_ends = jnp.cumsum(lengths).astype(jnp.int32)
    positions = jnp.arange(TOKENS_BIN, dtype=jnp.int32)
    segment = jnp.sum((positions[:, None] >= seg_ends[None, :]).astype(jnp.int32), axis=1)
    key_rows = bin_kv[:, :HEAD].astype(jnp.float32)
    value_rows = bin_kv[:, HEAD:].astype(jnp.float32)
    block_len = 512 if TOKENS_BIN % 512 == 0 else TOK_DEV
    count = TOKENS_BIN // block_len

    def one_block(block_no):
        first = (block_no * block_len).astype(jnp.int32)
        query_block = lax.dynamic_slice_in_dim(bin_q, first, block_len, 0).astype(jnp.float32)
        query_block = query_block.reshape(block_len, QPG, HEAD)
        query_pos = first + jnp.arange(block_len, dtype=jnp.int32)
        query_seg = lax.dynamic_slice_in_dim(segment, first, block_len, 0)
        visible = (positions[None, :] <= query_pos[:, None]) & (segment[None, :] == query_seg[:, None])
        scores = jnp.einsum("thd,sd->ths", query_block, key_rows, precision=lax.Precision.HIGHEST)
        scores = scores * (HEAD ** -0.5)
        scores = jnp.where(visible[:, None, :], scores, -jnp.inf)
        maxima = jnp.max(scores, axis=-1)
        weights = jnp.where(visible[:, None, :], jnp.exp(scores - maxima[..., None]), 0.0)
        totals = jnp.sum(weights, axis=-1)
        rounded = weights.astype(jnp.bfloat16).astype(jnp.float32)
        numer = jnp.einsum("ths,sd->thd", rounded, value_rows, precision=lax.Precision.HIGHEST)
        return (numer / totals[..., None]).astype(jnp.bfloat16).reshape(block_len, QPG * HEAD)

    blocks = lax.map(one_block, jnp.arange(count, dtype=jnp.int32))
    return blocks.reshape(TOKENS_BIN, QPG * HEAD)


def reference(queries, keyvals, dest_bin, source_owner, seq_lengths):
    targets = dest_bin.reshape(N_DP, N_CTX, TOK_DEV)
    sources = source_owner.reshape(N_DP, N_CTX, TOK_DEV)
    send_rank = rank_within(targets)
    take_rank = rank_within(sources)
    owner_grid = jnp.broadcast_to(jnp.arange(N_DP, dtype=jnp.int32)[:, None, None], targets.shape)
    block_grid = jnp.broadcast_to(jnp.arange(N_CTX, dtype=jnp.int32)[None, :, None], targets.shape)
    row_grid = jnp.broadcast_to(jnp.arange(TOK_DEV, dtype=jnp.int32)[None, None, :], targets.shape)
    flat_rows = owner_grid * TOKENS_BIN + block_grid * TOK_DEV + row_grid
    slot_rows = jnp.zeros((N_CTX, N_DP, N_DP, CAP), jnp.int32)
    slot_rows = slot_rows.at[block_grid, owner_grid, targets, send_rank].set(flat_rows)
    chosen = slot_rows[block_grid, sources, owner_grid, take_rank].reshape(-1).astype(jnp.int32)
    bin_q = queries.reshape(N_DP * TOKENS_BIN, QPG * HEAD)[chosen].reshape(N_DP, TOKENS_BIN, QPG * HEAD)
    bin_kv = keyvals.reshape(N_DP * TOKENS_BIN, 2 * HEAD)[chosen].reshape(N_DP, TOKENS_BIN, 2 * HEAD)
    return lax.map(attend_bin, (bin_q, bin_kv, seq_lengths))
```

```python
import functools

import jax
import jax.numpy as jnp
from jax import lax
from jax.experimental import pallas as pl
from jax.experimental.pallas import tpu as pltpu
from jax.sharding import PartitionSpec as P

LOG2E = 1.4426950408889634
LOW = -1e30


def slots_of(labels, owners, capacity):
    n = labels.shape[1]
    hot = lax.broadcasted_iota(jnp.int32, (owners, n), 0) == labels
    hot16 = jnp.where(hot, 1.0, 0.0).astype(jnp.bfloat16)
    earlier = lax.broadcasted_iota(jnp.int32, (n, n), 0) < lax.broadcasted_iota(
        jnp.int32, (n, n), 1
    )
    earlier16 = jnp.where(earlier, 1.0, 0.0).astype(jnp.bfloat16)
    before = jnp.dot(hot16, earlier16, preferred_element_type=jnp.float32)
    rank = jnp.sum(jnp.where(hot, before, 0.0), axis=0, keepdims=True)
    return labels * capacity + rank.astype(jnp.int32)


def pack_kernel(owners, capacity, dest_ref, rows_ref, out_ref):
    slots = slots_of(dest_ref[...], owners, capacity)
    n = slots.shape[1]
    hot = lax.broadcasted_iota(jnp.int32, (owners * capacity, n), 0) == slots
    picks = jnp.where(hot, 1.0, 0.0).astype(jnp.bfloat16)
    out_ref[...] = jnp.dot(
        picks, rows_ref[...], preferred_element_type=jnp.float32
    ).astype(out_ref.dtype)


def picks_of(source_ref, owners, capacity):
    slots = slots_of(source_ref[...], owners, capacity)
    n = slots.shape[1]
    wide = jnp.broadcast_to(slots.astype(jnp.float32), (128, n))
    tall = jnp.transpose(wide).astype(jnp.int32)
    lane = lax.broadcasted_iota(jnp.int32, (n, 128), 1)
    parts = [
        jnp.where(tall == lane + 128 * i, 1.0, 0.0).astype(jnp.bfloat16)
        for i in range(owners * capacity // 128)
    ]
    return jnp.concatenate(parts, axis=1)


def unpack_kernel(owners, capacity, source_ref, rows_ref, out_ref):
    picks = picks_of(source_ref, owners, capacity)
    out_ref[...] = jnp.dot(
        picks, rows_ref[...], preferred_element_type=jnp.float32
    ).astype(out_ref.dtype)


def attend_kernel(owners, capacity, head, reach, *refs):
    lengths_ref, source_ref, got_ref = refs[:3]
    blocks = refs[3 : 3 + 2 * reach]
    out_ref, kv, q_all, acc, top, total, sems = refs[3 + 2 * reach :]
    n = source_ref.shape[1]
    groups = out_ref.shape[1] // head
    chunk = 2 * n
    chips = kv.shape[0] // chunk
    me = lax.axis_index("ctx")
    chip = me // 2
    core = me - 2 * chip

    copies = []
    for d in range(reach):
        at = lax.rem(chip - d + chips, chips) * chunk
        for other in range(2):
            side = core if other == 0 else 1 - core
            first = pl.multiple_of(at + side * n, n)
            copy = pltpu.make_async_copy(
                blocks[2 * d + other], kv.at[pl.ds(first, n), :], sems.at[2 * d + other]
            )
            copy.start()
            copies.append(copy)

    picks = picks_of(source_ref, owners, capacity)
    q_all[...] = jnp.dot(
        picks, got_ref[...], preferred_element_type=jnp.float32
    ).astype(q_all.dtype)

    starts = [jnp.int32(0)]
    for i in range(lengths_ref.shape[1] - 1):
        starts.append(starts[-1] + lengths_ref[0, i])

    def start_of(position):
        found = jnp.zeros_like(position)
        for s in starts[1:]:
            found = jnp.where(position >= s, jnp.maximum(found, s), found)
        return found

    q_first = me * n
    q_pos = q_first + lax.broadcasted_iota(jnp.int32, (1, n), 1)
    q_start = start_of(q_pos)
    low = start_of(q_first) // chunk
    full = jnp.minimum((start_of(q_first + n - 1) + chunk - 1) // chunk, chip)
    scale = LOG2E * head ** (-0.5)

    for copy in copies:
        copy.wait()

    def step(k, masked, first):
        at = pl.multiple_of(k * chunk, chunk)
        keys = kv[pl.ds(at, chunk), :head]
        values = jnp.transpose(kv[pl.ds(at, chunk), head:])
        if masked:
            k_pos = at + lax.broadcasted_iota(jnp.int32, (chunk, n), 0)
            visible = (k_pos <= q_pos) & (k_pos >= q_start)
        for h in range(groups):
            q = q_all[:, h * head : (h + 1) * head]
            s = lax.dot_general(
                keys, q, (((1,), (1,)), ((), ())), preferred_element_type=jnp.float32
            ) * scale
            if masked:
                s = jnp.where(visible, s, LOW)
            s_top = jnp.max(s, axis=0, keepdims=True)
            new_top = s_top if first else jnp.maximum(top[h], s_top)
            w = jnp.exp2(s - new_top)
            w_sum = jnp.sum(w, axis=0, keepdims=True)
            part = jnp.dot(
                values, w.astype(jnp.bfloat16), preferred_element_type=jnp.float32
            )
            if first:
                total[h] = w_sum
                acc[h] = part
            else:
                fade = jnp.exp2(top[h] - new_top)
                total[h] = total[h] * fade + w_sum
                acc[h] = acc[h] * fade + part
            top[h] = new_top

    step(chip, True, True)

    @pl.loop(low, full)
    def _(k):
        step(k, True, False)

    @pl.loop(jnp.maximum(low, full), chip)
    def _(k):
        step(k, False, False)

    for h in range(groups):
        out_ref[:, h * head : (h + 1) * head] = jnp.transpose(acc[h] / total[h]).astype(
            out_ref.dtype
        )


def vmem(count):
    return [pl.BlockSpec(memory_space=pltpu.VMEM)] * count


def body(queries, keyvals, dest_bin, source_owner, seq_lengths):
    owners = lax.axis_size("dp")
    n_ctx = lax.axis_size("ctx")
    n = queries.shape[1]
    width = queries.shape[2]
    kv_width = keyvals.shape[2]
    head = kv_width // 2
    capacity = 2 * n // owners
    slots = owners * capacity

    def pack(rows):
        return pl.pallas_call(
            functools.partial(pack_kernel, owners, capacity),
            out_shape=jax.ShapeDtypeStruct((slots, rows.shape[1]), rows.dtype),
            in_specs=vmem(2),
            out_specs=vmem(1)[0],
            compiler_params=pltpu.CompilerParams(vmem_limit_bytes=12 << 20),
            cost_estimate=pl.CostEstimate(
                flops=2 * slots * n * rows.shape[1],
                bytes_accessed=6 * n * rows.shape[1],
                transcendentals=0,
            ),
        )(dest_bin, rows)

    def exchange(rows):
        return lax.all_to_all(
            rows.reshape(owners, capacity, rows.shape[1]),
            "dp",
            split_axis=0,
            concat_axis=0,
            tiled=True,
        ).reshape(slots, rows.shape[1])

    got_kv = exchange(pack(keyvals[0]))
    got_q = exchange(pack(queries[0]))
    own = pl.pallas_call(
        functools.partial(unpack_kernel, owners, capacity),
        out_shape=jax.ShapeDtypeStruct((n, kv_width), keyvals.dtype),
        in_specs=vmem(2),
        out_specs=vmem(1)[0],
        compiler_params=pltpu.CompilerParams(vmem_limit_bytes=12 << 20),
        cost_estimate=pl.CostEstimate(
            flops=2 * slots * n * kv_width, bytes_accessed=6 * n * kv_width, transcendentals=0
        ),
    )(source_owner, got_kv)

    def shift(x, by):
        return lax.ppermute(x, "ctx", [(c, (c + by) % n_ctx) for c in range(n_ctx)])

    def swap(x):
        return lax.ppermute(x, "ctx", [(c, c ^ 1) for c in range(n_ctx)])

    reach = 7
    same = [own]
    for _ in range(4):
        same.append(shift(same[-1], 2))
    same.append(shift(own, 10))
    same.append(shift(own, 12))
    blocks = []
    for x in same:
        blocks += [x, swap(x)]

    chunk = 2 * n
    attended = pl.pallas_call(
        functools.partial(attend_kernel, owners, capacity, head, reach),
        out_shape=jax.ShapeDtypeStruct((n, width), queries.dtype),
        in_specs=[pl.BlockSpec(memory_space=pltpu.SMEM)]
        + vmem(2)
        + [pl.BlockSpec(memory_space=pl.ANY)] * (2 * reach),
        out_specs=vmem(1)[0],
        scratch_shapes=[
            pltpu.VMEM((n_ctx * n, kv_width), keyvals.dtype),
            pltpu.VMEM((n, width), queries.dtype),
            pltpu.VMEM((width // head, head, n), jnp.float32),
            pltpu.VMEM((width // head, 1, n), jnp.float32),
            pltpu.VMEM((width // head, 1, n), jnp.float32),
            pltpu.SemaphoreType.DMA((2 * reach,)),
        ],
        compiler_params=pltpu.CompilerParams(vmem_limit_bytes=24 << 20),
        cost_estimate=pl.CostEstimate(
            flops=4 * n * width * 12 * n,
            bytes_accessed=8 * n * width,
            transcendentals=12 * n * n * width // head,
        ),
    )(seq_lengths, source_owner, got_q, *blocks)
    return attended.reshape(1, n, width)


def solution(mesh):
    return jax.shard_map(
        body,
        mesh=mesh,
        in_specs=(
            P("dp", "ctx", None),
            P("dp", "ctx", None),
            P("dp", "ctx"),
            P("dp", "ctx"),
            P("dp", None),
        ),
        out_specs=P("dp", "ctx", None),
        check_vma=False,
    )
```

```python
import functools

import jax
import jax.numpy as jnp
from jax import lax
from jax.experimental import pallas as pl
from jax.experimental.pallas import tpu as pltpu
from jax.sharding import PartitionSpec as P

LOG2E = 1.4426950408889634
LOW = -1e30


def slots_of(labels, owners, capacity):
    n = labels.shape[1]
    hot = lax.broadcasted_iota(jnp.int32, (owners, n), 0) == labels
    hot16 = jnp.where(hot, 1.0, 0.0).astype(jnp.bfloat16)
    earlier = lax.broadcasted_iota(jnp.int32, (n, n), 0) < lax.broadcasted_iota(
        jnp.int32, (n, n), 1
    )
    earlier16 = jnp.where(earlier, 1.0, 0.0).astype(jnp.bfloat16)
    before = jnp.dot(hot16, earlier16, preferred_element_type=jnp.float32)
    rank = jnp.sum(jnp.where(hot, before, 0.0), axis=0, keepdims=True)
    return labels * capacity + rank.astype(jnp.int32)


def pack_kernel(owners, capacity, dest_ref, rows_ref, out_ref):
    slots = slots_of(dest_ref[...], owners, capacity)
    n = slots.shape[1]
    hot = lax.broadcasted_iota(jnp.int32, (owners * capacity, n), 0) == slots
    picks = jnp.where(hot, 1.0, 0.0).astype(jnp.bfloat16)
    out_ref[...] = jnp.dot(
        picks, rows_ref[...], preferred_element_type=jnp.float32
    ).astype(out_ref.dtype)


def picks_of(source_ref, owners, capacity):
    slots = slots_of(source_ref[...], owners, capacity)
    n = slots.shape[1]
    wide = jnp.broadcast_to(slots.astype(jnp.float32), (128, n))
    tall = jnp.transpose(wide).astype(jnp.int32)
    lane = lax.broadcasted_iota(jnp.int32, (n, 128), 1)
    parts = [
        jnp.where(tall == lane + 128 * i, 1.0, 0.0).astype(jnp.bfloat16)
        for i in range(owners * capacity // 128)
    ]
    return jnp.concatenate(parts, axis=1)


def unpack_kernel(owners, capacity, source_ref, rows_ref, out_ref):
    picks = picks_of(source_ref, owners, capacity)
    out_ref[...] = jnp.dot(
        picks, rows_ref[...], preferred_element_type=jnp.float32
    ).astype(out_ref.dtype)


def join_kernel(own_ref, other_ref, out_ref):
    n = own_ref.shape[0]
    core = lax.rem(lax.axis_index("ctx"), 2)
    out_ref[pl.ds(pl.multiple_of(core * n, n), n), :] = own_ref[...]
    out_ref[pl.ds(pl.multiple_of((1 - core) * n, n), n), :] = other_ref[...]


def attend_kernel(owners, capacity, head, far, *refs):
    lengths_ref, source_ref, got_ref = refs[:3]
    near = refs[3 : 3 + len(far)]
    out_ref, kv, q_all, acc, top, over = refs[3 + len(far) :]
    n = source_ref.shape[1]
    groups = out_ref.shape[1] // head
    chunk = 2 * n
    me = lax.axis_index("ctx")
    chip = me // 2
    core = me - 2 * chip

    picks = picks_of(source_ref, owners, capacity)
    for h in range(groups):
        exact = jnp.dot(
            picks, got_ref[:, h * head : (h + 1) * head], preferred_element_type=jnp.float32
        ) * (LOG2E * head ** (-0.5))
        high = exact.astype(jnp.bfloat16)
        q_all[:, 2 * h * head : (2 * h + 1) * head] = high
        rest = exact - high.astype(jnp.float32)
        q_all[:, (2 * h + 1) * head : (2 * h + 2) * head] = rest.astype(jnp.bfloat16)

    starts = [jnp.int32(0)]
    for i in range(lengths_ref.shape[1] - 1):
        starts.append(starts[-1] + lengths_ref[0, i])

    def start_of(position):
        found = jnp.zeros_like(position)
        for s in starts[1:]:
            found = jnp.where(position >= s, jnp.maximum(found, s), found)
        return found

    q_first = me * n
    q_pos = q_first + lax.broadcasted_iota(jnp.int32, (1, n), 1)
    q_start = start_of(q_pos)
    low = start_of(q_first)
    high = start_of(q_first + n - 1)

    def distance(i):
        d = jnp.int32(0)
        for j, (a, b) in enumerate(far):
            d = jnp.where(i == j, jnp.where(core == 0, a, b), d)
        return d

    for i, (ref, (a, b)) in enumerate(zip(near, far)):
        at = (chip - jnp.where(core == 0, a, b)) * chunk

        @pl.when((at >= 0) & (at + chunk > low))
        def _():
            kv[i, :, :head] = ref[:, :head]
            kv[i, :, head:] = ref[:, head:]

    def tree_max(s):
        while s.shape[0] > 8:
            half = s.shape[0] // 2
            s = jnp.maximum(s[:half], s[half:])
        return jnp.max(s, axis=0, keepdims=True)

    def step(i, at, masked, mode):
        keys = jnp.concatenate([kv[i, :, :head]] * 2, axis=1)
        values = jnp.concatenate(
            [jnp.transpose(kv[i, :, head:]), jnp.ones((16, chunk), jnp.bfloat16)], axis=0
        )
        if masked:
            k_pos = at + lax.broadcasted_iota(jnp.int32, (chunk, n), 0)
            visible = (k_pos <= q_pos) & (k_pos >= q_start)

        def qk(h):
            s = lax.dot_general(
                keys,
                q_all[:, 2 * h * head : 2 * (h + 1) * head],
                (((1,), (1,)), ((), ())),
                preferred_element_type=jnp.float32,
            )
            return jnp.where(visible, s, LOW) if masked else s

        def soft(h, s):
            if mode == "fast":
                e = s - top[h]
                over[...] = jnp.maximum(over[...], tree_max(e))
                return jnp.exp2(e).astype(jnp.bfloat16), None
            if mode == "first":
                m = tree_max(s)
                top[h] = m
                return jnp.exp2(s - m).astype(jnp.bfloat16), None
            old = top[h]
            m = jnp.maximum(old, tree_max(s))
            top[h] = m
            return jnp.exp2(s - m).astype(jnp.bfloat16), jnp.exp2(old - m)

        def pv(h, w, fade):
            part = jnp.dot(values, w, preferred_element_type=jnp.float32)
            if mode == "fast":
                acc[h] += part
            elif mode == "first":
                acc[h] = part
            else:
                acc[h] = acc[h] * fade + part

        lag = 2
        s_of, w_of = {}, {}
        for t in range(groups + 1 + lag):
            if t < groups:
                s_of[t] = qk(t)
            if 0 <= t - 1 < groups:
                w_of[t - 1] = soft(t - 1, s_of.pop(t - 1))
            if 0 <= t - 1 - lag < groups:
                pv(t - 1 - lag, *w_of.pop(t - 1 - lag))

    def here(at):
        return (at >= 0) & (at + chunk > low)

    over[...] = jnp.full((1, n), LOW, jnp.float32)
    step(0, chip * chunk, True, "first")

    @pl.loop(1, len(far))
    def _(i):
        at = (chip - distance(i)) * chunk
        clear = (at >= high) & (at + chunk <= q_first)

        @pl.when(here(at) & clear)
        def _():
            step(i, at, False, "fast")

        @pl.when(here(at) & jnp.logical_not(clear))
        def _():
            step(i, at, True, "fast")

    @pl.when(jnp.max(over[...]) > 64.0)
    def _():
        for h in range(groups):
            top[h] = jnp.full((1, n), LOW, jnp.float32)
            acc[h] = jnp.zeros(acc.shape[1:], jnp.float32)

        @pl.loop(0, len(far))
        def _(i):
            at = (chip - distance(i)) * chunk

            @pl.when(here(at))
            def _():
                step(i, at, True, "slow")

    for h in range(groups):
        done = (acc[h, :head] * (1.0 / acc[h, head : head + 1])).astype(out_ref.dtype)
        out_ref[:, h * head : (h + 1) * head] = jnp.transpose(done)


def vmem(count):
    return [pl.BlockSpec(memory_space=pltpu.VMEM)] * count


def body(queries, keyvals, dest_bin, source_owner, seq_lengths):
    owners = lax.axis_size("dp")
    n_ctx = lax.axis_size("ctx")
    n = queries.shape[1]
    width = queries.shape[2]
    kv_width = keyvals.shape[2]
    head = kv_width // 2
    capacity = 2 * n // owners
    slots = owners * capacity

    def pack(rows):
        return pl.pallas_call(
            functools.partial(pack_kernel, owners, capacity),
            out_shape=jax.ShapeDtypeStruct((slots, rows.shape[1]), rows.dtype),
            in_specs=vmem(2),
            out_specs=vmem(1)[0],
            compiler_params=pltpu.CompilerParams(vmem_limit_bytes=12 << 20),
            cost_estimate=pl.CostEstimate(
                flops=2 * slots * n * rows.shape[1],
                bytes_accessed=6 * n * rows.shape[1],
                transcendentals=0,
            ),
        )(dest_bin, rows)

    def exchange(rows):
        return lax.all_to_all(
            rows.reshape(owners, capacity, rows.shape[1]),
            "dp",
            split_axis=0,
            concat_axis=0,
            tiled=True,
        ).reshape(slots, rows.shape[1])

    got_kv = exchange(pack(keyvals[0]))
    got_q = exchange(pack(queries[0]))
    own = pl.pallas_call(
        functools.partial(unpack_kernel, owners, capacity),
        out_shape=jax.ShapeDtypeStruct((n, kv_width), keyvals.dtype),
        in_specs=vmem(2),
        out_specs=vmem(1)[0],
        compiler_params=pltpu.CompilerParams(vmem_limit_bytes=12 << 20),
        cost_estimate=pl.CostEstimate(
            flops=2 * slots * n * kv_width, bytes_accessed=6 * n * kv_width, transcendentals=0
        ),
    )(source_owner, got_kv)

    def hop(x, up, down):
        return lax.ppermute(
            x,
            "ctx",
            [(c, (c + (2 * up if c % 2 == 0 else -2 * down)) % n_ctx) for c in range(n_ctx)],
        )

    def swap(x):
        return lax.ppermute(x, "ctx", [(c, c ^ 1) for c in range(n_ctx)])

    pair = pl.pallas_call(
        join_kernel,
        out_shape=jax.ShapeDtypeStruct((2 * n, kv_width), keyvals.dtype),
        in_specs=vmem(2),
        out_specs=vmem(1)[0],
        compiler_params=pltpu.CompilerParams(vmem_limit_bytes=4 << 20),
        cost_estimate=pl.CostEstimate(
            flops=0, bytes_accessed=8 * n * kv_width, transcendentals=0
        ),
    )(own, swap(own))
    hop1 = hop(pair, 1, 2)
    hop2 = hop(hop1, 1, 1)
    hop3 = hop(hop1, 2, 2)
    far = [(0, 0), (1, 6), (6, 1), (2, 5), (5, 2), (3, 4), (4, 3)]
    pieces = [pair, hop1, swap(hop1), hop2, swap(hop2), hop3, swap(hop3)]
    groups = width // head

    attended = pl.pallas_call(
        functools.partial(attend_kernel, owners, capacity, head, far),
        out_shape=jax.ShapeDtypeStruct((n, width), queries.dtype),
        in_specs=[pl.BlockSpec(memory_space=pltpu.SMEM)] + vmem(2 + len(far)),
        out_specs=vmem(1)[0],
        scratch_shapes=[
            pltpu.VMEM((len(far), 2 * n, kv_width), keyvals.dtype),
            pltpu.VMEM((n, 2 * width), queries.dtype),
            pltpu.VMEM((groups, head + 16, n), jnp.float32),
            pltpu.VMEM((groups, 1, n), jnp.float32),
            pltpu.VMEM((1, n), jnp.float32),
        ],
        compiler_params=pltpu.CompilerParams(vmem_limit_bytes=24 << 20),
        cost_estimate=pl.CostEstimate(
            flops=4 * n * width * 12 * n,
            bytes_accessed=8 * n * width,
            transcendentals=12 * n * n * groups,
        ),
    )(seq_lengths, source_owner, got_q, *pieces)
    return attended.reshape(1, n, width)


def solution(mesh):
    return jax.shard_map(
        body,
        mesh=mesh,
        in_specs=(
            P("dp", "ctx", None),
            P("dp", "ctx", None),
            P("dp", "ctx"),
            P("dp", "ctx"),
            P("dp", None),
        ),
        out_specs=P("dp", "ctx", None),
        check_vma=False,
    )
```

```python
import functools

import jax
import jax.numpy as jnp
from jax import lax
from jax.experimental import pallas as pl
from jax.experimental.pallas import tpu as pltpu
from jax.sharding import PartitionSpec as P


LOG2E = 1.4426950408889634
LOW = -1e30


def slots_of(labels, owners, capacity):
    n = labels.shape[1]
    hot = lax.broadcasted_iota(jnp.int32, (owners, n), 0) == labels
    hot16 = jnp.where(hot, 1.0, 0.0).astype(jnp.bfloat16)
    earlier = lax.broadcasted_iota(jnp.int32, (n, n), 0) < lax.broadcasted_iota(
        jnp.int32, (n, n), 1
    )
    earlier16 = jnp.where(earlier, 1.0, 0.0).astype(jnp.bfloat16)
    before = jnp.dot(hot16, earlier16, preferred_element_type=jnp.float32)
    rank = jnp.sum(jnp.where(hot, before, 0.0), axis=0, keepdims=True)
    return labels * capacity + rank.astype(jnp.int32)


def pack_kernel(owners, capacity, dest_ref, rows_ref, out_ref):
    slots = slots_of(dest_ref[...], owners, capacity)
    n = slots.shape[1]
    hot = lax.broadcasted_iota(jnp.int32, (owners * capacity, n), 0) == slots
    picks = jnp.where(hot, 1.0, 0.0).astype(jnp.bfloat16)
    out_ref[...] = jnp.dot(
        picks, rows_ref[...], preferred_element_type=jnp.float32
    ).astype(out_ref.dtype)


def picks_of(source_ref, owners, capacity):
    slots = slots_of(source_ref[...], owners, capacity)
    n = slots.shape[1]
    wide = jnp.broadcast_to(slots.astype(jnp.float32), (128, n))
    tall = jnp.transpose(wide).astype(jnp.int32)
    lane = lax.broadcasted_iota(jnp.int32, (n, 128), 1)
    parts = [
        jnp.where(tall == lane + 128 * i, 1.0, 0.0).astype(jnp.bfloat16)
        for i in range(owners * capacity // 128)
    ]
    return jnp.concatenate(parts, axis=1)


def picks_kernel(owners, capacity, source_ref, out_ref):
    out_ref[...] = picks_of(source_ref, owners, capacity)


def unpack_kernel(picks_ref, rows_ref, out_ref):
    out_ref[...] = jnp.dot(
        picks_ref[...], rows_ref[...], preferred_element_type=jnp.float32
    ).astype(out_ref.dtype)


def join_kernel(own_ref, other_ref, out_ref):
    n = own_ref.shape[0]
    core = lax.rem(lax.axis_index("ctx"), 2)
    out_ref[pl.ds(pl.multiple_of(core * n, n), n), :] = own_ref[...]
    out_ref[pl.ds(pl.multiple_of((1 - core) * n, n), n), :] = other_ref[...]


def attend_kernel(head, far, *refs):
    lengths_ref, picks_ref, got_ref = refs[:3]
    near = refs[3 : 3 + len(far)]
    out_ref, kv, q_all, acc, top, over = refs[3 + len(far) :]
    n = picks_ref.shape[0]
    groups = out_ref.shape[1] // head
    chunk = 2 * n
    me = lax.axis_index("ctx")
    chip = me // 2
    core = me - 2 * chip

    picks = picks_ref[...]
    for h in range(groups):
        exact = jnp.dot(
            picks, got_ref[:, h * head : (h + 1) * head], preferred_element_type=jnp.float32
        ) * (LOG2E * head ** (-0.5))
        high = exact.astype(jnp.bfloat16)
        q_all[:, 2 * h * head : (2 * h + 1) * head] = high
        rest = exact - high.astype(jnp.float32)
        q_all[:, (2 * h + 1) * head : (2 * h + 2) * head] = rest.astype(jnp.bfloat16)

    starts = [jnp.int32(0)]
    for i in range(lengths_ref.shape[1] - 1):
        starts.append(starts[-1] + lengths_ref[0, i])

    def start_of(position):
        found = jnp.zeros_like(position)
        for s in starts[1:]:
            found = jnp.where(position >= s, jnp.maximum(found, s), found)
        return found

    q_first = me * n
    q_pos = q_first + lax.broadcasted_iota(jnp.int32, (1, n), 1)
    q_start = start_of(q_pos)
    low = start_of(q_first)
    high = start_of(q_first + n - 1)

    def distance(i):
        d = jnp.int32(0)
        for j, (a, b) in enumerate(far):
            d = jnp.where(i == j, jnp.where(core == 0, a, b), d)
        return d

    for i, (ref, (a, b)) in enumerate(zip(near, far)):
        at = (chip - jnp.where(core == 0, a, b)) * chunk

        @pl.when((at >= 0) & (at + chunk > low))
        def _():
            kv[i, :, :head] = ref[:, :head]
            kv[i, :, head:] = ref[:, head:]

    def tree_max(s):
        while s.shape[0] > 8:
            half = s.shape[0] // 2
            s = jnp.maximum(s[:half], s[half:])
        return jnp.max(s, axis=0, keepdims=True)

    def step(i, at, masked, mode):
        keys = jnp.concatenate([kv[i, :, :head]] * 2, axis=1)
        values = jnp.concatenate(
            [jnp.transpose(kv[i, :, head:]), jnp.ones((16, chunk), jnp.bfloat16)], axis=0
        )
        if masked:
            k_pos = at + lax.broadcasted_iota(jnp.int32, (chunk, n), 0)
            visible = (k_pos <= q_pos) & (k_pos >= q_start)

        def qk(h):
            s = lax.dot_general(
                keys,
                q_all[:, 2 * h * head : 2 * (h + 1) * head],
                (((1,), (1,)), ((), ())),
                preferred_element_type=jnp.float32,
            )
            return jnp.where(visible, s, LOW) if masked else s

        def soft(h, s):
            if mode == "fast":
                e = s - top[h]
                over[...] = jnp.maximum(over[...], tree_max(e))
                return jnp.exp2(e).astype(jnp.bfloat16), None
            if mode == "first":
                m = tree_max(s)
                top[h] = m
                return jnp.exp2(s - m).astype(jnp.bfloat16), None
            old = top[h]
            m = jnp.maximum(old, tree_max(s))
            top[h] = m
            return jnp.exp2(s - m).astype(jnp.bfloat16), jnp.exp2(old - m)

        def pv(h, w, fade):
            part = jnp.dot(values, w, preferred_element_type=jnp.float32)
            if mode == "fast":
                acc[h] += part
            elif mode == "first":
                acc[h] = part
            else:
                acc[h] = acc[h] * fade + part

        lag = 2
        s_of, w_of = {}, {}
        for t in range(groups + 1 + lag):
            if t < groups:
                s_of[t] = qk(t)
            if 0 <= t - 1 < groups:
                w_of[t - 1] = soft(t - 1, s_of.pop(t - 1))
            if 0 <= t - 1 - lag < groups:
                pv(t - 1 - lag, *w_of.pop(t - 1 - lag))

    def here(at):
        return (at >= 0) & (at + chunk > low)

    over[...] = jnp.full((1, n), LOW, jnp.float32)
    step(0, chip * chunk, True, "first")

    @pl.loop(1, len(far))
    def _(i):
        at = (chip - distance(i)) * chunk
        clear = (at >= high) & (at + chunk <= q_first)

        @pl.when(here(at) & clear)
        def _():
            step(i, at, False, "fast")

        @pl.when(here(at) & jnp.logical_not(clear))
        def _():
            step(i, at, True, "fast")

    @pl.when(jnp.max(over[...]) > 64.0)
    def _():
        for h in range(groups):
            top[h] = jnp.full((1, n), LOW, jnp.float32)
            acc[h] = jnp.zeros(acc.shape[1:], jnp.float32)

        @pl.loop(0, len(far))
        def _(i):
            at = (chip - distance(i)) * chunk

            @pl.when(here(at))
            def _():
                step(i, at, True, "slow")

    for h in range(groups):
        done = (acc[h, :head] * (1.0 / acc[h, head : head + 1])).astype(out_ref.dtype)
        out_ref[:, h * head : (h + 1) * head] = jnp.transpose(done)


def vmem(count):
    return [pl.BlockSpec(memory_space=pltpu.VMEM)] * count


def body(queries, keyvals, dest_bin, source_owner, seq_lengths):
    owners = lax.axis_size("dp")
    n_ctx = lax.axis_size("ctx")
    n = queries.shape[1]
    width = queries.shape[2]
    kv_width = keyvals.shape[2]
    head = kv_width // 2
    capacity = 2 * n // owners
    slots = owners * capacity

    def pack(rows):
        return pl.pallas_call(
            functools.partial(pack_kernel, owners, capacity),
            out_shape=jax.ShapeDtypeStruct((slots, rows.shape[1]), rows.dtype),
            in_specs=vmem(2),
            out_specs=vmem(1)[0],
            cost_estimate=pl.CostEstimate(
                flops=2 * slots * n * rows.shape[1],
                bytes_accessed=6 * n * rows.shape[1],
                transcendentals=0,
            ),
        )(dest_bin, rows)

    def exchange(rows):
        return lax.all_to_all(
            rows.reshape(owners, capacity, rows.shape[1]),
            "dp",
            split_axis=0,
            concat_axis=0,
            tiled=True,
        ).reshape(slots, rows.shape[1])

    got_kv = exchange(pack(keyvals[0]))
    got_q = exchange(pack(queries[0]))
    picks = pl.pallas_call(
        functools.partial(picks_kernel, owners, capacity),
        out_shape=jax.ShapeDtypeStruct((n, slots), keyvals.dtype),
        in_specs=vmem(1),
        out_specs=vmem(1)[0],
        compiler_params=pltpu.CompilerParams(vmem_limit_bytes=4 << 20),
        cost_estimate=pl.CostEstimate(
            flops=2 * n * n * owners, bytes_accessed=2 * n * slots, transcendentals=0
        ),
    )(source_owner)
    own = pl.pallas_call(
        unpack_kernel,
        out_shape=jax.ShapeDtypeStruct((n, kv_width), keyvals.dtype),
        in_specs=vmem(2),
        out_specs=vmem(1)[0],
        compiler_params=pltpu.CompilerParams(vmem_limit_bytes=12 << 20),
        cost_estimate=pl.CostEstimate(
            flops=2 * slots * n * kv_width, bytes_accessed=6 * n * kv_width, transcendentals=0
        ),
    )(picks, got_kv)

    def hop(x, up, down):
        return lax.ppermute(
            x,
            "ctx",
            [(c, (c + (2 * up if c % 2 == 0 else -2 * down)) % n_ctx) for c in range(n_ctx)],
        )

    def swap(x):
        return lax.ppermute(x, "ctx", [(c, c ^ 1) for c in range(n_ctx)])

    pair = pl.pallas_call(
        join_kernel,
        out_shape=jax.ShapeDtypeStruct((2 * n, kv_width), keyvals.dtype),
        in_specs=vmem(2),
        out_specs=vmem(1)[0],
        compiler_params=pltpu.CompilerParams(vmem_limit_bytes=4 << 20),
        cost_estimate=pl.CostEstimate(
            flops=0, bytes_accessed=8 * n * kv_width, transcendentals=0
        ),
    )(own, swap(own))
    hop1 = hop(pair, 1, 2)
    hop2 = hop(hop1, 1, 1)
    hop3 = hop(hop1, 2, 2)
    far = [(0, 0), (1, 6), (6, 1), (2, 5), (5, 2), (3, 4), (4, 3)]
    pieces = [pair, hop1, swap(hop1), hop2, swap(hop2), hop3, swap(hop3)]
    groups = width // head

    attended = pl.pallas_call(
        functools.partial(attend_kernel, head, far),
        out_shape=jax.ShapeDtypeStruct((n, width), queries.dtype),
        in_specs=[pl.BlockSpec(memory_space=pltpu.SMEM)] + vmem(2 + len(far)),
        out_specs=vmem(1)[0],
        scratch_shapes=[
            pltpu.VMEM((len(far), 2 * n, kv_width), keyvals.dtype),
            pltpu.VMEM((n, 2 * width), queries.dtype),
            pltpu.VMEM((groups, head + 16, n), jnp.float32),
            pltpu.VMEM((groups, 1, n), jnp.float32),
            pltpu.VMEM((1, n), jnp.float32),
        ],
        compiler_params=pltpu.CompilerParams(vmem_limit_bytes=24 << 20),
        cost_estimate=pl.CostEstimate(
            flops=4 * n * width * 12 * n,
            bytes_accessed=8 * n * width,
            transcendentals=12 * n * n * groups,
        ),
    )(seq_lengths, picks, got_q, *pieces)
    return attended.reshape(1, n, width)


def solution(mesh):
    return jax.shard_map(
        body,
        mesh=mesh,
        in_specs=(
            P("dp", "ctx", None),
            P("dp", "ctx", None),
            P("dp", "ctx"),
            P("dp", "ctx"),
            P("dp", None),
        ),
        out_specs=P("dp", "ctx", None),
        check_vma=False,
    )
```

```python
import functools

import jax
import jax.numpy as jnp
from jax import lax
from jax.experimental import pallas as pl
from jax.experimental.pallas import tpu as pltpu
from jax.sharding import PartitionSpec as P


LOG2E = 1.4426950408889634
LOW = -1e30


def slots_of(labels, owners, capacity):
    n = labels.shape[1]
    hot = lax.broadcasted_iota(jnp.int32, (owners, n), 0) == labels
    hot16 = jnp.where(hot, 1.0, 0.0).astype(jnp.bfloat16)
    earlier = lax.broadcasted_iota(jnp.int32, (n, n), 0) < lax.broadcasted_iota(
        jnp.int32, (n, n), 1
    )
    earlier16 = jnp.where(earlier, 1.0, 0.0).astype(jnp.bfloat16)
    before = jnp.dot(hot16, earlier16, preferred_element_type=jnp.float32)
    rank = jnp.sum(jnp.where(hot, before, 0.0), axis=0, keepdims=True)
    return labels * capacity + rank.astype(jnp.int32)


def pack_kernel(owners, capacity, dest_ref, rows_ref, out_ref):
    slots = slots_of(dest_ref[...], owners, capacity)
    n = slots.shape[1]
    hot = lax.broadcasted_iota(jnp.int32, (owners * capacity, n), 0) == slots
    picks = jnp.where(hot, 1.0, 0.0).astype(jnp.bfloat16)
    out_ref[...] = jnp.dot(
        picks, rows_ref[...], preferred_element_type=jnp.float32
    ).astype(out_ref.dtype)


def picks_of(source_ref, owners, capacity):
    slots = slots_of(source_ref[...], owners, capacity)
    n = slots.shape[1]
    wide = jnp.broadcast_to(slots.astype(jnp.float32), (128, n))
    tall = jnp.transpose(wide).astype(jnp.int32)
    lane = lax.broadcasted_iota(jnp.int32, (n, 128), 1)
    parts = [
        jnp.where(tall == lane + 128 * i, 1.0, 0.0).astype(jnp.bfloat16)
        for i in range(owners * capacity // 128)
    ]
    return jnp.concatenate(parts, axis=1)


def picks_kernel(owners, capacity, source_ref, out_ref):
    out_ref[...] = picks_of(source_ref, owners, capacity)


def unpack_kernel(picks_ref, rows_ref, out_ref):
    out_ref[...] = jnp.dot(
        picks_ref[...], rows_ref[...], preferred_element_type=jnp.float32
    ).astype(out_ref.dtype)


def join_kernel(own_ref, other_ref, out_ref):
    n = own_ref.shape[0]
    core = lax.rem(lax.axis_index("ctx"), 2)
    out_ref[pl.ds(pl.multiple_of(core * n, n), n), :] = own_ref[...]
    out_ref[pl.ds(pl.multiple_of((1 - core) * n, n), n), :] = other_ref[...]


def attend_kernel(head, far, *refs):
    lengths_ref, picks_ref, got_ref = refs[:3]
    near = refs[3 : 3 + len(far)]
    out_ref, kv, q_all, acc, top, total = refs[3 + len(far) :]
    n = picks_ref.shape[0]
    groups = out_ref.shape[1] // head
    chunk = 2 * n
    me = lax.axis_index("ctx")
    chip = me // 2
    core = me - 2 * chip

    picks = picks_ref[...]
    for h in range(0, groups, 2):
        both = jnp.dot(
            picks, got_ref[:, h * head : (h + 2) * head], preferred_element_type=jnp.float32
        ) * (LOG2E * head ** (-0.5))
        for i in range(2):
            exact = both[:, i * head : (i + 1) * head]
            high = exact.astype(q_all.dtype)
            at = 2 * (h + i) * head
            q_all[:, at : at + head] = high
            q_all[:, at + head : at + 2 * head] = (exact - high.astype(jnp.float32)).astype(
                q_all.dtype
            )

    starts = [jnp.int32(0)]
    for i in range(lengths_ref.shape[1] - 1):
        starts.append(starts[-1] + lengths_ref[0, i])

    def start_of(position):
        found = jnp.zeros_like(position)
        for s in starts[1:]:
            found = jnp.where(position >= s, jnp.maximum(found, s), found)
        return found

    q_first = me * n
    q_pos = q_first + lax.broadcasted_iota(jnp.int32, (1, n), 1)
    q_start = start_of(q_pos)
    low = start_of(q_first)
    high = start_of(q_first + n - 1)

    def place(i):
        d = jnp.int32(0)
        for j, (a, b) in enumerate(far):
            d = jnp.where(i == j, jnp.where(core == 0, a, b), d)
        return (chip - d) * chunk

    def here(at):
        return (at >= 0) & (at + chunk > low)

    for i, ref in enumerate(near):

        @pl.when(here(place(i)))
        def _():
            kv[i] = ref[...]

    def tree_max(s):
        while s.shape[0] > 8:
            half = s.shape[0] // 2
            s = jnp.maximum(s[:half], s[half:])
        return jnp.max(s, axis=0, keepdims=True)

    def fold(w):
        return jnp.sum(w.reshape(-1, 8, w.shape[1]), axis=0)

    def step(i, at, first_row, rows, masked, mode):
        keys = jnp.concatenate([kv[i, first_row : first_row + rows, :head]] * 2, axis=1)
        values = jnp.transpose(kv[i, first_row : first_row + rows, head:])
        if masked:
            k_pos = at + first_row + lax.broadcasted_iota(jnp.int32, (rows, n), 0)
            visible = (k_pos <= q_pos) & (k_pos >= q_start)

        def scores(h):
            s = lax.dot_general(
                keys,
                q_all[:, 2 * h * head : 2 * (h + 1) * head],
                (((1,), (1,)), ((), ())),
                preferred_element_type=jnp.float32,
            )
            return jnp.where(visible, s, LOW) if masked else s

        def weigh(h, s):
            fade = None
            if mode == "fixed":
                m = top[h]
            elif mode == "first":
                m = tree_max(s)
                top[h] = m
            else:
                old = top[h]
                m = jnp.maximum(old, tree_max(s))
                top[h] = m
                fade = jnp.exp2(old - m)
            w = jnp.exp2(s - m)
            if mode == "fixed":
                total[h] += fold(w)
            elif mode == "first":
                total[h] = fold(w)
            else:
                total[h] = total[h] * fade + fold(w)
            return w.astype(kv.dtype), fade

        def gather(h, w, fade):
            part = jnp.dot(values, w, preferred_element_type=jnp.float32)
            if mode == "fixed":
                acc[h] += part
            elif mode == "first":
                acc[h] = part
            else:
                acc[h] = acc[h] * fade + part

        lag = 2
        s_of, w_of = {}, {}
        for t in range(groups + 1 + lag):
            if t < groups:
                s_of[t] = scores(t)
            if 0 <= t - 1 < groups:
                w_of[t - 1] = weigh(t - 1, s_of.pop(t - 1))
            if 0 <= t - 1 - lag < groups:
                gather(t - 1 - lag, *w_of.pop(t - 1 - lag))

    own = chip * chunk

    @pl.when(core == 0)
    def _():
        step(0, own, 0, n, True, "first")

    @pl.when(core != 0)
    def _():
        step(0, own, 0, chunk, True, "first")

    @pl.loop(1, len(far))
    def _(i):
        at = place(i)
        clear = (at >= high) & (at + chunk <= q_first)
        late = low >= at + n

        @pl.when(here(at) & clear)
        def _():
            step(i, at, 0, chunk, False, "fixed")

        @pl.when(here(at) & jnp.logical_not(clear) & late)
        def _():
            step(i, at, n, n, True, "fixed")

        @pl.when(here(at) & jnp.logical_not(clear | late))
        def _():
            step(i, at, 0, chunk, True, "fixed")

    most = total[0]
    for h in range(1, groups):
        most = jnp.maximum(most, total[h])

    @pl.when(jnp.max(most) > 2.0**64)
    def _():
        for h in range(groups):
            top[h] = jnp.full((1, n), LOW, jnp.float32)
            total[h] = jnp.zeros(total.shape[1:], jnp.float32)
            acc[h] = jnp.zeros(acc.shape[1:], jnp.float32)

        @pl.loop(0, len(far))
        def _(i):
            at = place(i)

            @pl.when(here(at))
            def _():
                step(i, at, 0, chunk, True, "running")

    for h in range(groups):
        share = 1.0 / jnp.sum(total[h], axis=0, keepdims=True)
        out_ref[:, h * head : (h + 1) * head] = jnp.transpose(
            (acc[h] * share).astype(out_ref.dtype)
        )


def vmem(count):
    return [pl.BlockSpec(memory_space=pltpu.VMEM)] * count


def body(queries, keyvals, dest_bin, source_owner, seq_lengths):
    owners = lax.axis_size("dp")
    n_ctx = lax.axis_size("ctx")
    n = queries.shape[1]
    width = queries.shape[2]
    kv_width = keyvals.shape[2]
    head = kv_width // 2
    capacity = 2 * n // owners
    slots = owners * capacity

    def pack(rows):
        return pl.pallas_call(
            functools.partial(pack_kernel, owners, capacity),
            out_shape=jax.ShapeDtypeStruct((slots, rows.shape[1]), rows.dtype),
            in_specs=vmem(2),
            out_specs=vmem(1)[0],
            cost_estimate=pl.CostEstimate(
                flops=2 * slots * n * rows.shape[1],
                bytes_accessed=6 * n * rows.shape[1],
                transcendentals=0,
            ),
        )(dest_bin, rows)

    def exchange(rows):
        return lax.all_to_all(
            rows.reshape(owners, capacity, rows.shape[1]),
            "dp",
            split_axis=0,
            concat_axis=0,
            tiled=True,
        ).reshape(slots, rows.shape[1])

    got_kv = exchange(pack(keyvals[0]))
    got_q = exchange(pack(queries[0]))
    picks = pl.pallas_call(
        functools.partial(picks_kernel, owners, capacity),
        out_shape=jax.ShapeDtypeStruct((n, slots), keyvals.dtype),
        in_specs=vmem(1),
        out_specs=vmem(1)[0],
        compiler_params=pltpu.CompilerParams(vmem_limit_bytes=4 << 20),
        cost_estimate=pl.CostEstimate(
            flops=2 * n * n * owners, bytes_accessed=2 * n * slots, transcendentals=0
        ),
    )(source_owner)
    own = pl.pallas_call(
        unpack_kernel,
        out_shape=jax.ShapeDtypeStruct((n, kv_width), keyvals.dtype),
        in_specs=vmem(2),
        out_specs=vmem(1)[0],
        compiler_params=pltpu.CompilerParams(vmem_limit_bytes=12 << 20),
        cost_estimate=pl.CostEstimate(
            flops=2 * slots * n * kv_width, bytes_accessed=6 * n * kv_width, transcendentals=0
        ),
    )(picks, got_kv)

    def hop(x, up, down):
        return lax.ppermute(
            x,
            "ctx",
            [(c, (c + (2 * up if c % 2 == 0 else -2 * down)) % n_ctx) for c in range(n_ctx)],
        )

    def swap(x):
        return lax.ppermute(x, "ctx", [(c, c ^ 1) for c in range(n_ctx)])

    pair = pl.pallas_call(
        join_kernel,
        out_shape=jax.ShapeDtypeStruct((2 * n, kv_width), keyvals.dtype),
        in_specs=vmem(2),
        out_specs=vmem(1)[0],
        compiler_params=pltpu.CompilerParams(vmem_limit_bytes=4 << 20),
        cost_estimate=pl.CostEstimate(
            flops=0, bytes_accessed=8 * n * kv_width, transcendentals=0
        ),
    )(own, swap(own))
    hop1 = hop(pair, 1, 2)
    hop2 = hop(hop1, 1, 1)
    hop3 = hop(hop1, 2, 2)
    far = [(0, 0), (1, 6), (6, 1), (2, 5), (5, 2), (3, 4), (4, 3)]
    pieces = [pair, hop1, swap(hop1), hop2, swap(hop2), hop3, swap(hop3)]
    groups = width // head

    attended = pl.pallas_call(
        functools.partial(attend_kernel, head, far),
        out_shape=jax.ShapeDtypeStruct((n, width), queries.dtype),
        in_specs=[pl.BlockSpec(memory_space=pltpu.SMEM)] + vmem(2 + len(far)),
        out_specs=vmem(1)[0],
        scratch_shapes=[
            pltpu.VMEM((len(far), 2 * n, kv_width), keyvals.dtype),
            pltpu.VMEM((n, 2 * width), queries.dtype),
            pltpu.VMEM((groups, head, n), jnp.float32),
            pltpu.VMEM((groups, 1, n), jnp.float32),
            pltpu.VMEM((groups, 8, n), jnp.float32),
        ],
        compiler_params=pltpu.CompilerParams(vmem_limit_bytes=24 << 20),
        cost_estimate=pl.CostEstimate(
            flops=4 * n * width * 12 * n,
            bytes_accessed=8 * n * width,
            transcendentals=12 * n * n * groups,
        ),
    )(seq_lengths, picks, got_q, *pieces)
    return attended.reshape(1, n, width)


def solution(mesh):
    return jax.shard_map(
        body,
        mesh=mesh,
        in_specs=(
            P("dp", "ctx", None),
            P("dp", "ctx", None),
            P("dp", "ctx"),
            P("dp", "ctx"),
            P("dp", None),
        ),
        out_specs=P("dp", "ctx", None),
        check_vma=False,
    )
```

```python
import functools
import typing

import jax
import jax.numpy as jnp
from jax import lax
from jax.experimental import pallas as pl
from jax.experimental.pallas import tpu as pltpu
from jax.sharding import PartitionSpec as P


LOG2E = 1.4426950408889634
LOW = -1e30


def slots_of(labels, owners, capacity):
    n = labels.shape[1]
    hot = lax.broadcasted_iota(jnp.int32, (owners, n), 0) == labels
    hot16 = jnp.where(hot, 1.0, 0.0).astype(jnp.bfloat16)
    earlier = lax.broadcasted_iota(jnp.int32, (n, n), 0) < lax.broadcasted_iota(
        jnp.int32, (n, n), 1
    )
    earlier16 = jnp.where(earlier, 1.0, 0.0).astype(jnp.bfloat16)
    before = jnp.dot(hot16, earlier16, preferred_element_type=jnp.float32)
    rank = jnp.sum(jnp.where(hot, before, 0.0), axis=0, keepdims=True)
    return labels * capacity + rank.astype(jnp.int32)


def pack_kernel(owners, capacity, dest_ref, rows_ref, out_ref):
    slots = slots_of(dest_ref[...], owners, capacity)
    n = slots.shape[1]
    hot = lax.broadcasted_iota(jnp.int32, (owners * capacity, n), 0) == slots
    picks = jnp.where(hot, 1.0, 0.0).astype(jnp.bfloat16)
    out_ref[...] = jnp.dot(
        picks, rows_ref[...], preferred_element_type=jnp.float32
    ).astype(out_ref.dtype)


def picks_of(source_ref, owners, capacity):
    slots = slots_of(source_ref[...], owners, capacity)
    n = slots.shape[1]
    wide = jnp.broadcast_to(slots.astype(jnp.float32), (128, n))
    tall = jnp.transpose(wide).astype(jnp.int32)
    lane = lax.broadcasted_iota(jnp.int32, (n, 128), 1)
    parts = [
        jnp.where(tall == lane + 128 * i, 1.0, 0.0).astype(jnp.bfloat16)
        for i in range(owners * capacity // 128)
    ]
    return jnp.concatenate(parts, axis=1)


def picks_kernel(owners, capacity, source_ref, out_ref):
    out_ref[...] = picks_of(source_ref, owners, capacity)


def unpack_kernel(picks_ref, rows_ref, out_ref):
    out_ref[...] = jnp.dot(
        picks_ref[...], rows_ref[...], preferred_element_type=jnp.float32
    ).astype(out_ref.dtype)


def join_kernel(own_ref, other_ref, out_ref):
    n = own_ref.shape[0]
    core = lax.rem(lax.axis_index("ctx"), 2)
    out_ref[pl.ds(pl.multiple_of(core * n, n), n), :] = own_ref[...]
    out_ref[pl.ds(pl.multiple_of((1 - core) * n, n), n), :] = other_ref[...]


def split_query(head, picks, got_ref, q_all):
    groups = got_ref.shape[1] // head
    for h in range(0, groups, 2):
        both = jnp.dot(
            picks, got_ref[:, h * head : (h + 2) * head], preferred_element_type=jnp.float32
        ) * (LOG2E * head ** (-0.5))
        for i in range(2):
            exact = both[:, i * head : (i + 1) * head]
            high = exact.astype(q_all.dtype)
            at = 2 * (h + i) * head
            q_all[:, at : at + head] = high
            q_all[:, at + head : at + 2 * head] = (exact - high.astype(jnp.float32)).astype(
                q_all.dtype
            )


class Block(typing.NamedTuple):
    core: jax.Array
    own: jax.Array
    place: typing.Callable
    here: typing.Callable
    clear: typing.Callable
    late: typing.Callable
    step: typing.Callable


def block_of(head, far, lengths_ref, kv, q_all, acc, top, total):
    n = q_all.shape[0]
    groups = acc.shape[0]
    chunk = 2 * n
    me = lax.axis_index("ctx")
    chip = me // 2
    core = me - 2 * chip

    starts = [jnp.int32(0)]
    for i in range(lengths_ref.shape[1] - 1):
        starts.append(starts[-1] + lengths_ref[0, i])

    def start_of(position):
        found = jnp.zeros_like(position)
        for s in starts[1:]:
            found = jnp.where(position >= s, jnp.maximum(found, s), found)
        return found

    q_first = me * n
    q_pos = q_first + lax.broadcasted_iota(jnp.int32, (1, n), 1)
    q_start = start_of(q_pos)
    low = start_of(q_first)
    high = start_of(q_first + n - 1)

    def place(i):
        return (chip - jnp.where(core == 0, far[i][0], far[i][1])) * chunk

    def here(at):
        return (at >= 0) & (at + chunk > low)

    def clear(at):
        return (at >= high) & (at + chunk <= q_first)

    def late(at):
        return low >= at + n

    def tree_max(s):
        while s.shape[0] > 8:
            half = s.shape[0] // 2
            s = jnp.maximum(s[:half], s[half:])
        return jnp.max(s, axis=0, keepdims=True)

    def fold(w):
        return jnp.sum(w.reshape(-1, 8, w.shape[1]), axis=0)

    def step(row, rows, position, masked, mode):
        row = pl.multiple_of(row, n)
        keys = jnp.concatenate([kv[pl.ds(row, rows), :head]] * 2, axis=1)
        values = jnp.transpose(kv[pl.ds(row, rows), head:])
        if masked:
            k_pos = position + lax.broadcasted_iota(jnp.int32, (rows, n), 0)
            visible = (k_pos <= q_pos) & (k_pos >= q_start)

        def scores(h):
            s = lax.dot_general(
                keys,
                q_all[:, 2 * h * head : 2 * (h + 1) * head],
                (((1,), (1,)), ((), ())),
                preferred_element_type=jnp.float32,
            )
            return jnp.where(visible, s, LOW) if masked else s

        def weigh(h, s):
            fade = None
            if mode == "fixed":
                m = top[h]
            elif mode == "first":
                m = tree_max(s)
                top[h] = m
            else:
                old = top[h]
                m = jnp.maximum(old, tree_max(s))
                top[h] = m
                fade = jnp.exp2(old - m)
            w = jnp.exp2(s - m)
            if mode == "fixed":
                total[h] += fold(w)
            elif mode == "first":
                total[h] = fold(w)
            else:
                total[h] = total[h] * fade + fold(w)
            return w.astype(kv.dtype), fade

        def gather(h, w, fade):
            part = jnp.dot(values, w, preferred_element_type=jnp.float32)
            if mode == "fixed":
                acc[h] += part
            elif mode == "first":
                acc[h] = part
            else:
                acc[h] = acc[h] * fade + part

        lag = 2
        s_of, w_of = {}, {}
        for t in range(groups + 1 + lag):
            if t < groups:
                s_of[t] = scores(t)
            if 0 <= t - 1 < groups:
                w_of[t - 1] = weigh(t - 1, s_of.pop(t - 1))
            if 0 <= t - 1 - lag < groups:
                gather(t - 1 - lag, *w_of.pop(t - 1 - lag))

    return Block(core, chip * chunk, place, here, clear, late, step)


def attend_kernel(head, far, *refs):
    lengths_ref, picks_ref, got_ref = refs[:3]
    near = refs[3:-6]
    q_all, acc, top, total, kv, at_of = refs[-6:]
    n = picks_ref.shape[0]
    chunk = 2 * n
    split_query(head, picks_ref[...], got_ref, q_all)
    block = block_of(head, far, lengths_ref, kv, q_all, acc, top, total)

    last = len(near) - 1
    kv[0:chunk] = near[0][...]
    plain = jnp.int32(0)
    edged = jnp.int32(0)
    for i in range(1, len(near)):
        at = block.place(i)
        is_here = block.here(at)
        is_clear = block.clear(at)
        slot = jnp.where(is_clear, 1 + plain, last - edged)

        @pl.when(is_here)
        def _():
            kv[pl.ds(pl.multiple_of(slot * chunk, chunk), chunk)] = near[i][...]
            at_of[slot] = at

        plain += jnp.where(is_here & is_clear, 1, 0)
        edged += jnp.where(is_here & jnp.logical_not(is_clear), 1, 0)

    @pl.when(block.core == 0)
    def _():
        block.step(0, n, block.own, True, "first")

    @pl.when(block.core != 0)
    def _():
        block.step(0, chunk, block.own, True, "first")

    @pl.loop(0, plain // 2)
    def _(p):
        block.step((1 + 2 * p) * chunk, 2 * chunk, 0, False, "fixed")

    @pl.when(lax.rem(plain, 2) == 1)
    def _():
        block.step(plain * chunk, chunk, 0, False, "fixed")

    @pl.loop(0, edged)
    def _(j):
        slot = last - j
        at = at_of[slot]

        @pl.when(block.late(at))
        def _():
            block.step(slot * chunk + n, n, at + n, True, "fixed")

        @pl.when(jnp.logical_not(block.late(at)))
        def _():
            block.step(slot * chunk, chunk, at, True, "fixed")


def finish_kernel(head, far, *refs):
    lengths_ref, q_all, acc_ref, top_ref, total_ref = refs[:5]
    near = refs[5:-5]
    out_ref, kv, acc, top, total = refs[-5:]
    n = q_all.shape[0]
    groups = acc.shape[0]
    chunk = 2 * n
    acc[...] = acc_ref[...]
    top[...] = top_ref[...]
    total[...] = total_ref[...]
    block = block_of(head, far, lengths_ref, kv, q_all, acc, top, total)
    at = block.place(len(near) - 1)
    is_here = block.here(at)
    is_clear = block.clear(at)
    is_late = block.late(at)

    @pl.when(is_here)
    def _():
        kv[...] = near[-1][...]

    @pl.when(is_here & is_clear)
    def _():
        block.step(0, chunk, at, False, "fixed")

    @pl.when(is_here & jnp.logical_not(is_clear) & is_late)
    def _():
        block.step(n, n, at + n, True, "fixed")

    @pl.when(is_here & jnp.logical_not(is_clear | is_late))
    def _():
        block.step(0, chunk, at, True, "fixed")

    most = total[0]
    for h in range(1, groups):
        most = jnp.maximum(most, total[h])

    @pl.when(jnp.max(most) > 2.0**64)
    def _():
        for h in range(groups):
            top[h] = jnp.full((1, n), LOW, jnp.float32)
            total[h] = jnp.zeros(total.shape[1:], jnp.float32)
            acc[h] = jnp.zeros(acc.shape[1:], jnp.float32)

        @pl.loop(0, len(near))
        def _(i):
            place = block.place(0)
            for j, ref in enumerate(near):
                place = jnp.where(i == j, block.place(j), place)

                @pl.when(i == j)
                def _():
                    kv[...] = ref[...]

            @pl.when(block.here(place))
            def _():
                block.step(0, chunk, place, True, "running")

    for h in range(groups):
        share = 1.0 / jnp.sum(total[h], axis=0, keepdims=True)
        out_ref[:, h * head : (h + 1) * head] = jnp.transpose(
            (acc[h] * share).astype(out_ref.dtype)
        )


def vmem(count):
    return [pl.BlockSpec(memory_space=pltpu.VMEM)] * count


def body(queries, keyvals, dest_bin, source_owner, seq_lengths):
    owners = lax.axis_size("dp")
    n_ctx = lax.axis_size("ctx")
    n = queries.shape[1]
    width = queries.shape[2]
    kv_width = keyvals.shape[2]
    head = kv_width // 2
    capacity = 2 * n // owners
    slots = owners * capacity

    def pack(rows):
        return pl.pallas_call(
            functools.partial(pack_kernel, owners, capacity),
            out_shape=jax.ShapeDtypeStruct((slots, rows.shape[1]), rows.dtype),
            in_specs=vmem(2),
            out_specs=vmem(1)[0],
            cost_estimate=pl.CostEstimate(
                flops=2 * slots * n * rows.shape[1],
                bytes_accessed=6 * n * rows.shape[1],
                transcendentals=0,
            ),
        )(dest_bin, rows)

    def exchange(rows):
        return lax.all_to_all(
            rows.reshape(owners, capacity, rows.shape[1]),
            "dp",
            split_axis=0,
            concat_axis=0,
            tiled=True,
        ).reshape(slots, rows.shape[1])

    got_kv = exchange(pack(keyvals[0]))
    got_q = exchange(pack(queries[0]))
    picks = pl.pallas_call(
        functools.partial(picks_kernel, owners, capacity),
        out_shape=jax.ShapeDtypeStruct((n, slots), keyvals.dtype),
        in_specs=vmem(1),
        out_specs=vmem(1)[0],
        compiler_params=pltpu.CompilerParams(vmem_limit_bytes=4 << 20),
        cost_estimate=pl.CostEstimate(
            flops=2 * n * n * owners, bytes_accessed=2 * n * slots, transcendentals=0
        ),
    )(source_owner)
    own = pl.pallas_call(
        unpack_kernel,
        out_shape=jax.ShapeDtypeStruct((n, kv_width), keyvals.dtype),
        in_specs=vmem(2),
        out_specs=vmem(1)[0],
        compiler_params=pltpu.CompilerParams(vmem_limit_bytes=12 << 20),
        cost_estimate=pl.CostEstimate(
            flops=2 * slots * n * kv_width, bytes_accessed=6 * n * kv_width, transcendentals=0
        ),
    )(picks, got_kv)

    def hop(x, up, down):
        return lax.ppermute(
            x,
            "ctx",
            [(c, (c + (2 * up if c % 2 == 0 else -2 * down)) % n_ctx) for c in range(n_ctx)],
        )

    def swap(x):
        return lax.ppermute(x, "ctx", [(c, c ^ 1) for c in range(n_ctx)])

    pair = pl.pallas_call(
        join_kernel,
        out_shape=jax.ShapeDtypeStruct((2 * n, kv_width), keyvals.dtype),
        in_specs=vmem(2),
        out_specs=vmem(1)[0],
        compiler_params=pltpu.CompilerParams(vmem_limit_bytes=4 << 20),
        cost_estimate=pl.CostEstimate(
            flops=0, bytes_accessed=8 * n * kv_width, transcendentals=0
        ),
    )(own, swap(own))
    hop1 = hop(pair, 1, 2)
    hop2 = hop(hop1, 1, 1)
    hop3 = hop(hop1, 2, 2)
    far = [(0, 0), (1, 6), (6, 1), (2, 5), (5, 2), (3, 4), (4, 3)]
    last = swap(hop3)
    pieces = [pair, hop1, swap(hop1), hop2, swap(hop2), hop3, last]
    groups = width // head
    state = (
        jax.ShapeDtypeStruct((n, 2 * width), queries.dtype),
        jax.ShapeDtypeStruct((groups, head, n), jnp.float32),
        jax.ShapeDtypeStruct((groups, 1, n), jnp.float32),
        jax.ShapeDtypeStruct((groups, 8, n), jnp.float32),
    )

    sums = pl.pallas_call(
        functools.partial(attend_kernel, head, far),
        out_shape=state,
        in_specs=[pl.BlockSpec(memory_space=pltpu.SMEM)] + vmem(1 + len(far)),
        out_specs=tuple(vmem(len(state))),
        scratch_shapes=[
            pltpu.VMEM((2 * n * (len(far) - 1), kv_width), keyvals.dtype),
            pltpu.SMEM((len(far),), jnp.int32),
        ],
        compiler_params=pltpu.CompilerParams(vmem_limit_bytes=24 << 20),
        cost_estimate=pl.CostEstimate(
            flops=4 * n * width * 10 * n,
            bytes_accessed=8 * n * width,
            transcendentals=10 * n * n * groups,
        ),
    )(seq_lengths, picks, got_q, *pieces[:-1])
    attended = pl.pallas_call(
        functools.partial(finish_kernel, head, far),
        out_shape=jax.ShapeDtypeStruct((n, width), queries.dtype),
        in_specs=[pl.BlockSpec(memory_space=pltpu.SMEM)] + vmem(len(state) + len(far)),
        out_specs=vmem(1)[0],
        scratch_shapes=[
            pltpu.VMEM((2 * n, kv_width), keyvals.dtype),
            pltpu.VMEM(state[1].shape, jnp.float32),
            pltpu.VMEM(state[2].shape, jnp.float32),
            pltpu.VMEM(state[3].shape, jnp.float32),
        ],
        compiler_params=pltpu.CompilerParams(vmem_limit_bytes=24 << 20),
        cost_estimate=pl.CostEstimate(
            flops=4 * n * width * 2 * n,
            bytes_accessed=8 * n * width,
            transcendentals=2 * n * n * groups,
        ),
    )(seq_lengths, *sums, *pieces)
    return attended.reshape(1, n, width)


def solution(mesh):
    return jax.shard_map(
        body,
        mesh=mesh,
        in_specs=(
            P("dp", "ctx", None),
            P("dp", "ctx", None),
            P("dp", "ctx"),
            P("dp", "ctx"),
            P("dp", None),
        ),
        out_specs=P("dp", "ctx", None),
        check_vma=False,
    )
```

```python
import functools
import typing

import jax
import jax.numpy as jnp
from jax import lax
from jax.experimental import pallas as pl
from jax.experimental.pallas import tpu as pltpu
from jax.sharding import PartitionSpec as P


LOG2E = 1.4426950408889634
LOW = -1e30


def slots_of(labels, owners, capacity):
    n = labels.shape[1]
    hot = lax.broadcasted_iota(jnp.int32, (owners, n), 0) == labels
    hot16 = jnp.where(hot, 1.0, 0.0).astype(jnp.bfloat16)
    earlier = lax.broadcasted_iota(jnp.int32, (n, n), 0) < lax.broadcasted_iota(
        jnp.int32, (n, n), 1
    )
    earlier16 = jnp.where(earlier, 1.0, 0.0).astype(jnp.bfloat16)
    before = jnp.dot(hot16, earlier16, preferred_element_type=jnp.float32)
    rank = jnp.sum(jnp.where(hot, before, 0.0), axis=0, keepdims=True)
    return labels * capacity + rank.astype(jnp.int32)


def pack_kernel(owners, capacity, dest_hbm, rows_hbm, out_hbm, dest, rows, packed, sems):
    slots = owners * capacity
    n = rows.shape[0]
    fetch_dest = pltpu.make_async_copy(dest_hbm, dest, sems.at[0])
    fetch_rows = pltpu.make_async_copy(rows_hbm, rows, sems.at[1])
    fetch_dest.start()
    fetch_rows.start()
    fetch_dest.wait()
    slot = slots_of(dest[...], owners, capacity)
    half = slots // 2
    hot = [
        half * i + lax.broadcasted_iota(jnp.int32, (half, n), 0) == slot for i in range(2)
    ]
    picks = [jnp.where(h, 1.0, 0.0).astype(jnp.bfloat16) for h in hot]
    fetch_rows.wait()
    puts = []
    for i in range(2):
        part = pl.ds(half * i, half)
        packed[part, :] = jnp.dot(
            picks[i], rows[...], preferred_element_type=jnp.float32
        ).astype(packed.dtype)
        puts.append(
            pltpu.make_async_copy(packed.at[part, :], out_hbm.at[part, :], sems.at[2 + i])
        )
        puts[i].start()
    for put in puts:
        put.wait()


def picks_of(source_ref, owners, capacity):
    slots = slots_of(source_ref[...], owners, capacity)
    n = slots.shape[1]
    wide = jnp.broadcast_to(slots.astype(jnp.float32), (128, n))
    tall = jnp.transpose(wide).astype(jnp.int32)
    lane = lax.broadcasted_iota(jnp.int32, (n, 128), 1)
    parts = [
        jnp.where(tall == lane + 128 * i, 1.0, 0.0).astype(jnp.bfloat16)
        for i in range(owners * capacity // 128)
    ]
    return jnp.concatenate(parts, axis=1)


def picks_kernel(owners, capacity, source_ref, out_ref):
    out_ref[...] = picks_of(source_ref, owners, capacity)


def unpack_kernel(picks_ref, rows_ref, out_ref):
    out_ref[...] = jnp.dot(
        picks_ref[...], rows_ref[...], preferred_element_type=jnp.float32
    ).astype(out_ref.dtype)


def join_kernel(own_ref, other_ref, out_ref):
    n = own_ref.shape[0]
    core = lax.rem(lax.axis_index("ctx"), 2)
    out_ref[pl.ds(pl.multiple_of(core * n, n), n), :] = own_ref[...]
    out_ref[pl.ds(pl.multiple_of((1 - core) * n, n), n), :] = other_ref[...]


def split_query(head, picks, got_ref, q_all):
    groups = got_ref.shape[1] // head
    for h in range(0, groups, 2):
        both = jnp.dot(
            picks, got_ref[:, h * head : (h + 2) * head], preferred_element_type=jnp.float32
        ) * (LOG2E * head ** (-0.5))
        for i in range(2):
            exact = both[:, i * head : (i + 1) * head]
            high = exact.astype(q_all.dtype)
            at = 2 * (h + i) * head
            q_all[:, at : at + head] = high
            q_all[:, at + head : at + 2 * head] = (exact - high.astype(jnp.float32)).astype(
                q_all.dtype
            )


class Block(typing.NamedTuple):
    core: jax.Array
    own: jax.Array
    place: typing.Callable
    here: typing.Callable
    clear: typing.Callable
    late: typing.Callable
    step: typing.Callable


def block_of(head, far, lengths_ref, kv, q_all, acc, top, total):
    n = q_all.shape[0]
    groups = acc.shape[0]
    chunk = 2 * n
    me = lax.axis_index("ctx")
    chip = me // 2
    core = me - 2 * chip

    starts = [jnp.int32(0)]
    for i in range(lengths_ref.shape[1] - 1):
        starts.append(starts[-1] + lengths_ref[0, i])

    def start_of(position):
        found = jnp.zeros_like(position)
        for s in starts[1:]:
            found = jnp.where(position >= s, jnp.maximum(found, s), found)
        return found

    q_first = me * n
    q_pos = q_first + lax.broadcasted_iota(jnp.int32, (1, n), 1)
    q_start = start_of(q_pos)
    low = start_of(q_first)
    high = start_of(q_first + n - 1)

    def place(i):
        return (chip - jnp.where(core == 0, far[i][0], far[i][1])) * chunk

    def here(at):
        return (at >= 0) & (at + chunk > low)

    def clear(at):
        return (at >= high) & (at + chunk <= q_first)

    def late(at):
        return low >= at + n

    def tree_max(s):
        while s.shape[0] > 8:
            half = s.shape[0] // 2
            s = jnp.maximum(s[:half], s[half:])
        return jnp.max(s, axis=0, keepdims=True)

    def fold(w):
        return jnp.sum(w.reshape(-1, 8, w.shape[1]), axis=0)

    def step(row, rows, position, masked, mode):
        row = pl.multiple_of(row, n)
        keys = jnp.concatenate([kv[pl.ds(row, rows), :head]] * 2, axis=1)
        values = jnp.transpose(kv[pl.ds(row, rows), head:])
        if masked:
            k_pos = position + lax.broadcasted_iota(jnp.int32, (rows, n), 0)
            visible = (k_pos <= q_pos) & (k_pos >= q_start)

        def scores(h):
            s = lax.dot_general(
                keys,
                q_all[:, 2 * h * head : 2 * (h + 1) * head],
                (((1,), (1,)), ((), ())),
                preferred_element_type=jnp.float32,
            )
            return jnp.where(visible, s, LOW) if masked else s

        def weigh(h, s):
            fade = None
            if mode == "fixed":
                m = top[h]
            elif mode == "first":
                m = tree_max(s)
                top[h] = m
            else:
                old = top[h]
                m = jnp.maximum(old, tree_max(s))
                top[h] = m
                fade = jnp.exp2(old - m)
            w = jnp.exp2(s - m)
            if mode == "fixed":
                total[h] += fold(w)
            elif mode == "first":
                total[h] = fold(w)
            else:
                total[h] = total[h] * fade + fold(w)
            return w.astype(kv.dtype), fade

        def gather(h, w, fade):
            part = jnp.dot(values, w, preferred_element_type=jnp.float32)
            if mode == "fixed":
                acc[h] += part
            elif mode == "first":
                acc[h] = part
            else:
                acc[h] = acc[h] * fade + part

        lag = 2
        s_of, w_of = {}, {}
        for t in range(groups + 1 + lag):
            if t < groups:
                s_of[t] = scores(t)
            if 0 <= t - 1 < groups:
                w_of[t - 1] = weigh(t - 1, s_of.pop(t - 1))
            if 0 <= t - 1 - lag < groups:
                gather(t - 1 - lag, *w_of.pop(t - 1 - lag))

    return Block(core, chip * chunk, place, here, clear, late, step)


def attend_kernel(head, far, *refs):
    lengths_ref, picks_ref, got_ref = refs[:3]
    near = refs[3:-9]
    out_ref, kv, q_all, acc, top, total, done, at_of, sems = refs[-9:]
    n = picks_ref.shape[0]
    groups = acc.shape[0]
    chunk = 2 * n
    split_query(head, picks_ref[...], got_ref, q_all)
    block = block_of(head, far, lengths_ref, kv, q_all, acc, top, total)

    last = len(near) - 1
    kv[0:chunk] = near[0][...]
    plain = jnp.int32(0)
    edged = jnp.int32(0)
    for i in range(1, len(near)):
        at = block.place(i)
        is_here = block.here(at)
        is_clear = block.clear(at)
        slot = jnp.where(is_clear, 1 + plain, last - edged)

        @pl.when(is_here)
        def _():
            kv[pl.ds(pl.multiple_of(slot * chunk, chunk), chunk)] = near[i][...]
            at_of[slot] = at

        plain += jnp.where(is_here & is_clear, 1, 0)
        edged += jnp.where(is_here & jnp.logical_not(is_clear), 1, 0)

    @pl.when(block.core == 0)
    def _():
        block.step(0, n, block.own, True, "first")

    @pl.when(block.core != 0)
    def _():
        block.step(0, chunk, block.own, True, "first")

    @pl.loop(0, plain // 2)
    def _(p):
        block.step((1 + 2 * p) * chunk, 2 * chunk, 0, False, "fixed")

    @pl.when(lax.rem(plain, 2) == 1)
    def _():
        block.step(plain * chunk, chunk, 0, False, "fixed")

    @pl.loop(0, edged)
    def _(j):
        slot = last - j
        at = at_of[slot]

        @pl.when(block.late(at))
        def _():
            block.step(slot * chunk + n, n, at + n, True, "fixed")

        @pl.when(jnp.logical_not(block.late(at)))
        def _():
            block.step(slot * chunk, chunk, at, True, "fixed")

    most = total[0]
    for h in range(1, groups):
        most = jnp.maximum(most, total[h])

    @pl.when(jnp.max(most) > 2.0**64)
    def _():
        for h in range(groups):
            top[h] = jnp.full((1, n), LOW, jnp.float32)
            total[h] = jnp.zeros(total.shape[1:], jnp.float32)
            acc[h] = jnp.zeros(acc.shape[1:], jnp.float32)

        @pl.loop(0, len(near))
        def _(i):
            at = block.place(0)
            for j, ref in enumerate(near):
                at = jnp.where(i == j, block.place(j), at)

                @pl.when(i == j)
                def _():
                    kv[0:chunk] = ref[...]

            @pl.when(block.here(at))
            def _():
                block.step(0, chunk, at, True, "running")

    copies = []
    for h in range(groups):
        columns = pl.ds(h * head, head)
        share = 1.0 / jnp.sum(total[h], axis=0, keepdims=True)
        done[:, columns] = jnp.transpose((acc[h] * share).astype(done.dtype))
        copies.append(
            pltpu.make_async_copy(done.at[:, columns], out_ref.at[:, columns], sems.at[h])
        )
        copies[-1].start()
    for copy in copies:
        copy.wait()


def vmem(count):
    return [pl.BlockSpec(memory_space=pltpu.VMEM)] * count


def body(queries, keyvals, dest_bin, source_owner, seq_lengths):
    owners = lax.axis_size("dp")
    n_ctx = lax.axis_size("ctx")
    n = queries.shape[1]
    width = queries.shape[2]
    kv_width = keyvals.shape[2]
    head = kv_width // 2
    capacity = 2 * n // owners
    slots = owners * capacity

    def pack(rows):
        return pl.pallas_call(
            functools.partial(pack_kernel, owners, capacity),
            out_shape=jax.ShapeDtypeStruct((slots, rows.shape[1]), rows.dtype),
            in_specs=[pl.BlockSpec(memory_space=pl.ANY)] * 2,
            out_specs=pl.BlockSpec(memory_space=pl.ANY),
            scratch_shapes=[
                pltpu.VMEM(dest_bin.shape, dest_bin.dtype),
                pltpu.VMEM(rows.shape, rows.dtype),
                pltpu.VMEM((slots, rows.shape[1]), rows.dtype),
                pltpu.SemaphoreType.DMA((4,)),
            ],
            cost_estimate=pl.CostEstimate(
                flops=2 * slots * n * rows.shape[1],
                bytes_accessed=6 * n * rows.shape[1],
                transcendentals=0,
            ),
        )(dest_bin, rows)

    def exchange(rows):
        return lax.all_to_all(
            rows.reshape(owners, capacity, rows.shape[1]),
            "dp",
            split_axis=0,
            concat_axis=0,
            tiled=True,
        ).reshape(slots, rows.shape[1])

    got_kv = exchange(pack(keyvals[0]))
    got_q = exchange(pack(queries[0]))
    picks = pl.pallas_call(
        functools.partial(picks_kernel, owners, capacity),
        out_shape=jax.ShapeDtypeStruct((n, slots), keyvals.dtype),
        in_specs=vmem(1),
        out_specs=vmem(1)[0],
        compiler_params=pltpu.CompilerParams(vmem_limit_bytes=4 << 20),
        cost_estimate=pl.CostEstimate(
            flops=2 * n * n * owners, bytes_accessed=2 * n * slots, transcendentals=0
        ),
    )(source_owner)
    own = pl.pallas_call(
        unpack_kernel,
        out_shape=jax.ShapeDtypeStruct((n, kv_width), keyvals.dtype),
        in_specs=vmem(2),
        out_specs=vmem(1)[0],
        compiler_params=pltpu.CompilerParams(vmem_limit_bytes=12 << 20),
        cost_estimate=pl.CostEstimate(
            flops=2 * slots * n * kv_width, bytes_accessed=6 * n * kv_width, transcendentals=0
        ),
    )(picks, got_kv)

    def hop(x, up, down):
        return lax.ppermute(
            x,
            "ctx",
            [(c, (c + (2 * up if c % 2 == 0 else -2 * down)) % n_ctx) for c in range(n_ctx)],
        )

    def swap(x):
        return lax.ppermute(x, "ctx", [(c, c ^ 1) for c in range(n_ctx)])

    pair = pl.pallas_call(
        join_kernel,
        out_shape=jax.ShapeDtypeStruct((2 * n, kv_width), keyvals.dtype),
        in_specs=vmem(2),
        out_specs=vmem(1)[0],
        compiler_params=pltpu.CompilerParams(vmem_limit_bytes=4 << 20),
        cost_estimate=pl.CostEstimate(
            flops=0, bytes_accessed=8 * n * kv_width, transcendentals=0
        ),
    )(own, swap(own))
    hop1 = hop(pair, 1, 2)
    hop2 = hop(hop1, 1, 1)
    hop3 = hop(hop1, 2, 2)
    far = [(0, 0), (1, 6), (6, 1), (2, 5), (5, 2), (3, 4), (4, 3)]
    pieces = [pair, hop1, swap(hop1), hop2, swap(hop2), hop3, swap(hop3)]
    groups = width // head

    attended = pl.pallas_call(
        functools.partial(attend_kernel, head, far),
        out_shape=jax.ShapeDtypeStruct((n, width), queries.dtype),
        in_specs=[pl.BlockSpec(memory_space=pltpu.SMEM)] + vmem(2 + len(far)),
        out_specs=pl.BlockSpec(memory_space=pl.ANY),
        scratch_shapes=[
            pltpu.VMEM((2 * n * len(far), kv_width), keyvals.dtype),
            pltpu.VMEM((n, 2 * width), queries.dtype),
            pltpu.VMEM((groups, head, n), jnp.float32),
            pltpu.VMEM((groups, 1, n), jnp.float32),
            pltpu.VMEM((groups, 8, n), jnp.float32),
            pltpu.VMEM((n, width), queries.dtype),
            pltpu.SMEM((len(far),), jnp.int32),
            pltpu.SemaphoreType.DMA((groups,)),
        ],
        compiler_params=pltpu.CompilerParams(vmem_limit_bytes=28 << 20),
        cost_estimate=pl.CostEstimate(
            flops=4 * n * width * 12 * n,
            bytes_accessed=8 * n * width,
            transcendentals=12 * n * n * groups,
        ),
    )(seq_lengths, picks, got_q, *pieces)
    return attended.reshape(1, n, width)


def solution(mesh):
    return jax.shard_map(
        body,
        mesh=mesh,
        in_specs=(
            P("dp", "ctx", None),
            P("dp", "ctx", None),
            P("dp", "ctx"),
            P("dp", "ctx"),
            P("dp", None),
        ),
        out_specs=P("dp", "ctx", None),
        check_vma=False,
    )
```

```python
import functools
import typing

import jax
import jax.numpy as jnp
from jax import lax
from jax.experimental import pallas as pl
from jax.experimental.pallas import tpu as pltpu
from jax.sharding import PartitionSpec as P


LOG2E = 1.4426950408889634
LOW = -1e30


def slots_of(labels, owners, capacity):
    n = labels.shape[1]
    hot = lax.broadcasted_iota(jnp.int32, (owners, n), 0) == labels
    hot16 = jnp.where(hot, 1.0, 0.0).astype(jnp.bfloat16)
    earlier = lax.broadcasted_iota(jnp.int32, (n, n), 0) < lax.broadcasted_iota(
        jnp.int32, (n, n), 1
    )
    earlier16 = jnp.where(earlier, 1.0, 0.0).astype(jnp.bfloat16)
    before = jnp.dot(hot16, earlier16, preferred_element_type=jnp.float32)
    rank = jnp.sum(jnp.where(hot, before, 0.0), axis=0, keepdims=True)
    return labels * capacity + rank.astype(jnp.int32)


def pack_kernel(owners, capacity, dest_hbm, rows_hbm, out_hbm, dest, rows, packed, sems):
    slots = owners * capacity
    n = rows.shape[0]
    fetch_dest = pltpu.make_async_copy(dest_hbm, dest, sems.at[0])
    fetch_rows = pltpu.make_async_copy(rows_hbm, rows, sems.at[1])
    fetch_dest.start()
    fetch_rows.start()
    fetch_dest.wait()
    slot = slots_of(dest[...], owners, capacity)
    half = slots // 2
    hot = [
        half * i + lax.broadcasted_iota(jnp.int32, (half, n), 0) == slot for i in range(2)
    ]
    picks = [jnp.where(h, 1.0, 0.0).astype(jnp.bfloat16) for h in hot]
    fetch_rows.wait()
    puts = []
    for i in range(2):
        part = pl.ds(half * i, half)
        packed[part, :] = jnp.dot(
            picks[i], rows[...], preferred_element_type=jnp.float32
        ).astype(packed.dtype)
        puts.append(
            pltpu.make_async_copy(packed.at[part, :], out_hbm.at[part, :], sems.at[2 + i])
        )
        puts[i].start()
    for put in puts:
        put.wait()


def picks_of(source_ref, owners, capacity):
    slots = slots_of(source_ref[...], owners, capacity)
    n = slots.shape[1]
    wide = jnp.broadcast_to(slots.astype(jnp.float32), (128, n))
    tall = jnp.transpose(wide).astype(jnp.int32)
    lane = lax.broadcasted_iota(jnp.int32, (n, 128), 1)
    parts = [
        jnp.where(tall == lane + 128 * i, 1.0, 0.0).astype(jnp.bfloat16)
        for i in range(owners * capacity // 128)
    ]
    return jnp.concatenate(parts, axis=1)


def picks_kernel(owners, capacity, source_ref, out_ref):
    out_ref[...] = picks_of(source_ref, owners, capacity)


def unpack_kernel(picks_ref, rows_ref, out_ref):
    out_ref[...] = jnp.dot(
        picks_ref[...], rows_ref[...], preferred_element_type=jnp.float32
    ).astype(out_ref.dtype)


def join_kernel(own_ref, other_ref, out_ref):
    n = own_ref.shape[0]
    core = lax.rem(lax.axis_index("ctx"), 2)
    out_ref[pl.ds(pl.multiple_of(core * n, n), n), :] = own_ref[...]
    out_ref[pl.ds(pl.multiple_of((1 - core) * n, n), n), :] = other_ref[...]


def split_query(head, picks, got_ref, q_all):
    groups = got_ref.shape[1] // head
    for h in range(0, groups, 2):
        both = jnp.dot(
            picks, got_ref[:, h * head : (h + 2) * head], preferred_element_type=jnp.float32
        ) * (LOG2E * head ** (-0.5))
        for i in range(2):
            exact = both[:, i * head : (i + 1) * head]
            high = exact.astype(q_all.dtype)
            at = 2 * (h + i) * head
            q_all[:, at : at + head] = high
            q_all[:, at + head : at + 2 * head] = (exact - high.astype(jnp.float32)).astype(
                q_all.dtype
            )


class Block(typing.NamedTuple):
    core: jax.Array
    own: jax.Array
    place: typing.Callable
    here: typing.Callable
    clear: typing.Callable
    late: typing.Callable
    step: typing.Callable


def block_of(head, far, lengths_ref, kv, q_all, acc, top, total):
    n = q_all.shape[0]
    groups = acc.shape[0]
    chunk = 2 * n
    me = lax.axis_index("ctx")
    chip = me // 2
    core = me - 2 * chip

    starts = [jnp.int32(0)]
    for i in range(lengths_ref.shape[1] - 1):
        starts.append(starts[-1] + lengths_ref[0, i])

    def start_of(position):
        found = jnp.zeros_like(position)
        for s in starts[1:]:
            found = jnp.where(position >= s, jnp.maximum(found, s), found)
        return found

    q_first = me * n
    q_pos = q_first + lax.broadcasted_iota(jnp.int32, (1, n), 1)
    q_start = start_of(q_pos)
    low = start_of(q_first)
    high = start_of(q_first + n - 1)

    def place(i):
        return (chip - jnp.where(core == 0, far[i][0], far[i][1])) * chunk

    def here(at):
        return (at >= 0) & (at + chunk > low)

    def clear(at):
        return (at >= high) & (at + chunk <= q_first)

    def late(at):
        return low >= at + n

    def tree_max(s):
        while s.shape[0] > 8:
            half = s.shape[0] // 2
            s = jnp.maximum(s[:half], s[half:])
        return jnp.max(s, axis=0, keepdims=True)

    def fold(w):
        return jnp.sum(w.reshape(-1, 8, w.shape[1]), axis=0)

    def step(row, rows, position, masked, mode):
        row = pl.multiple_of(row, n)
        keys = jnp.concatenate([kv[pl.ds(row, rows), :head]] * 2, axis=1)
        values = jnp.transpose(kv[pl.ds(row, rows), head:])
        if masked:
            k_pos = position + lax.broadcasted_iota(jnp.int32, (rows, n), 0)
            visible = (k_pos <= q_pos) & (k_pos >= q_start)

        def scores(h):
            s = lax.dot_general(
                keys,
                q_all[:, 2 * h * head : 2 * (h + 1) * head],
                (((1,), (1,)), ((), ())),
                preferred_element_type=jnp.float32,
            )
            return jnp.where(visible, s, LOW) if masked else s

        def weigh(h, s):
            fade = None
            if mode == "fixed":
                m = top[h]
            elif mode == "first":
                m = tree_max(s)
                top[h] = m
            else:
                old = top[h]
                m = jnp.maximum(old, tree_max(s))
                top[h] = m
                fade = jnp.exp2(old - m)
            w = jnp.exp2(s - m)
            if mode == "fixed":
                total[h] += fold(w)
            elif mode == "first":
                total[h] = fold(w)
            else:
                total[h] = total[h] * fade + fold(w)
            return w.astype(kv.dtype), fade

        def gather(h, w, fade):
            part = jnp.dot(values, w, preferred_element_type=jnp.float32)
            if mode == "fixed":
                acc[h] += part
            elif mode == "first":
                acc[h] = part
            else:
                acc[h] = acc[h] * fade + part

        lag = 2
        s_of, w_of = {}, {}
        for t in range(groups + 1 + lag):
            if t < groups:
                s_of[t] = scores(t)
            if 0 <= t - 1 < groups:
                w_of[t - 1] = weigh(t - 1, s_of.pop(t - 1))
            if 0 <= t - 1 - lag < groups:
                gather(t - 1 - lag, *w_of.pop(t - 1 - lag))

    return Block(core, chip * chunk, place, here, clear, late, step)


def part_kernel(head, far, first, final, *refs):
    lengths_ref = refs[0]
    if first:
        picks_ref, got_ref = refs[1:3]
        near = refs[3 : 3 + len(far)]
        q_all, acc, top, total, kv = refs[3 + len(far) :]
        split_query(head, picks_ref[...], got_ref, q_all)
    else:
        q_all, acc_ref, top_ref, total_ref = refs[1:5]
        near = refs[5 : 5 + len(far)]
        if final:
            out_ref, kv, acc, top, total, done, sems = refs[5 + len(far) :]
            top[...] = top_ref[...]
        else:
            acc, total, kv = refs[5 + len(far) :]
            top = top_ref
        acc[...] = acc_ref[...]
        total[...] = total_ref[...]
    n = q_all.shape[0]
    groups = acc.shape[0]
    chunk = 2 * n
    block = block_of(head, far, lengths_ref, kv, q_all, acc, top, total)

    def place(i, count):
        at = block.place(0)
        for j in range(1, count):
            at = jnp.where(i == j, block.place(j), at)
        return at

    skip = 1 if first else 0
    fresh = kv.shape[0] // chunk
    names = far[:fresh]
    for i in range(len(names)):

        @pl.when(block.here(block.place(i)))
        def _():
            kv[i * chunk : (i + 1) * chunk] = near[i][...]

    if first:

        @pl.when(block.core == 0)
        def _():
            block.step(0, n, block.own, True, "first")

        @pl.when(block.core != 0)
        def _():
            block.step(0, chunk, block.own, True, "first")

    @pl.loop(skip, len(names))
    def _(i):
        at = place(i, len(names))
        is_here = block.here(at)
        is_clear = block.clear(at)
        is_late = block.late(at)

        @pl.when(is_here & is_clear)
        def _():
            block.step(i * chunk, chunk, at, False, "fixed")

        @pl.when(is_here & jnp.logical_not(is_clear) & is_late)
        def _():
            block.step(i * chunk + n, n, at + n, True, "fixed")

        @pl.when(is_here & jnp.logical_not(is_clear | is_late))
        def _():
            block.step(i * chunk, chunk, at, True, "fixed")

    if not final:
        return

    most = total[0]
    for h in range(1, groups):
        most = jnp.maximum(most, total[h])

    @pl.when(jnp.max(most) > 2.0**64)
    def _():
        for h in range(groups):
            top[h] = jnp.full((1, n), LOW, jnp.float32)
            total[h] = jnp.zeros(total.shape[1:], jnp.float32)
            acc[h] = jnp.zeros(acc.shape[1:], jnp.float32)

        @pl.loop(0, len(far))
        def _(t):
            i = len(far) - 1 - t
            at = place(i, len(far))
            for j, ref in enumerate(near):

                @pl.when(i == j)
                def _():
                    kv[0:chunk] = ref[...]

            @pl.when(block.here(at))
            def _():
                block.step(0, chunk, at, True, "running")

    copies = []
    for h in range(groups):
        columns = pl.ds(h * head, head)
        share = 1.0 / jnp.sum(total[h], axis=0, keepdims=True)
        done[:, columns] = jnp.transpose((acc[h] * share).astype(done.dtype))
        copies.append(
            pltpu.make_async_copy(done.at[:, columns], out_ref.at[:, columns], sems.at[h])
        )
        copies[-1].start()
    for copy in copies:
        copy.wait()


def vmem(count):
    return [pl.BlockSpec(memory_space=pltpu.VMEM)] * count


def body(queries, keyvals, dest_bin, source_owner, seq_lengths):
    owners = lax.axis_size("dp")
    n_ctx = lax.axis_size("ctx")
    n = queries.shape[1]
    width = queries.shape[2]
    kv_width = keyvals.shape[2]
    head = kv_width // 2
    capacity = 2 * n // owners
    slots = owners * capacity

    def pack(rows):
        return pl.pallas_call(
            functools.partial(pack_kernel, owners, capacity),
            out_shape=jax.ShapeDtypeStruct((slots, rows.shape[1]), rows.dtype),
            in_specs=[pl.BlockSpec(memory_space=pl.ANY)] * 2,
            out_specs=pl.BlockSpec(memory_space=pl.ANY),
            scratch_shapes=[
                pltpu.VMEM(dest_bin.shape, dest_bin.dtype),
                pltpu.VMEM(rows.shape, rows.dtype),
                pltpu.VMEM((slots, rows.shape[1]), rows.dtype),
                pltpu.SemaphoreType.DMA((4,)),
            ],
            cost_estimate=pl.CostEstimate(
                flops=2 * slots * n * rows.shape[1],
                bytes_accessed=6 * n * rows.shape[1],
                transcendentals=0,
            ),
        )(dest_bin, rows)

    def exchange(rows):
        return lax.all_to_all(
            rows.reshape(owners, capacity, rows.shape[1]),
            "dp",
            split_axis=0,
            concat_axis=0,
            tiled=True,
        ).reshape(slots, rows.shape[1])

    got_kv = exchange(pack(keyvals[0]))
    got_q = exchange(pack(queries[0]))
    picks = pl.pallas_call(
        functools.partial(picks_kernel, owners, capacity),
        out_shape=jax.ShapeDtypeStruct((n, slots), keyvals.dtype),
        in_specs=vmem(1),
        out_specs=vmem(1)[0],
        compiler_params=pltpu.CompilerParams(vmem_limit_bytes=4 << 20),
        cost_estimate=pl.CostEstimate(
            flops=2 * n * n * owners, bytes_accessed=2 * n * slots, transcendentals=0
        ),
    )(source_owner)
    own = pl.pallas_call(
        unpack_kernel,
        out_shape=jax.ShapeDtypeStruct((n, kv_width), keyvals.dtype),
        in_specs=vmem(2),
        out_specs=vmem(1)[0],
        compiler_params=pltpu.CompilerParams(vmem_limit_bytes=12 << 20),
        cost_estimate=pl.CostEstimate(
            flops=2 * slots * n * kv_width,
            bytes_accessed=6 * n * kv_width,
            transcendentals=0,
        ),
    )(picks, got_kv)

    def hop(x, up, down):
        return lax.ppermute(
            x,
            "ctx",
            [(c, (c + (2 * up if c % 2 == 0 else -2 * down)) % n_ctx) for c in range(n_ctx)],
        )

    def swap(x):
        return lax.ppermute(x, "ctx", [(c, c ^ 1) for c in range(n_ctx)])

    pair = pl.pallas_call(
        join_kernel,
        out_shape=jax.ShapeDtypeStruct((2 * n, kv_width), keyvals.dtype),
        in_specs=vmem(2),
        out_specs=vmem(1)[0],
        compiler_params=pltpu.CompilerParams(vmem_limit_bytes=4 << 20),
        cost_estimate=pl.CostEstimate(
            flops=0, bytes_accessed=8 * n * kv_width, transcendentals=0
        ),
    )(own, swap(own))
    hop1 = hop(pair, 1, 2)
    hop2 = hop(hop1, 1, 1)
    hop3 = hop(hop1, 2, 2)
    groups = width // head
    query = jax.ShapeDtypeStruct((n, 2 * width), queries.dtype)
    sums = jax.ShapeDtypeStruct((groups, head, n), jnp.float32)
    tops = jax.ShapeDtypeStruct((groups, 1, n), jnp.float32)
    totals = jax.ShapeDtypeStruct((groups, 8, n), jnp.float32)

    def attend(pieces, fresh, inputs, outputs, scratch, first=False, final=False):
        return pl.pallas_call(
            functools.partial(part_kernel, head, [f for f, _ in pieces], first, final),
            out_shape=outputs,
            in_specs=[pl.BlockSpec(memory_space=pltpu.SMEM)] + vmem(len(inputs) + len(pieces)),
            out_specs=pl.BlockSpec(memory_space=pl.ANY) if final else tuple(vmem(len(outputs))),
            scratch_shapes=[pltpu.VMEM((2 * n * fresh, kv_width), keyvals.dtype)] + scratch,
            compiler_params=pltpu.CompilerParams(vmem_limit_bytes=20 << 20),
            cost_estimate=pl.CostEstimate(
                flops=8 * n * n * width * fresh,
                bytes_accessed=8 * n * width,
                transcendentals=2 * n * n * groups * fresh,
            ),
        )(seq_lengths, *inputs, *[x for _, x in pieces])

    swapped1 = swap(hop1)
    early = [((0, 0), pair), ((1, 6), hop1), ((6, 1), swapped1)]
    middle = [((2, 5), hop2), ((5, 2), swap(hop2))]
    late = [((3, 4), hop3), ((4, 3), swap(hop3))]
    q_all, acc, top, total = attend(
        early, 3, (picks, got_q), (query, sums, tops, totals), [], first=True
    )
    acc, total = attend(middle, 2, (q_all, acc, top, total), (sums, totals), [])
    attended = attend(
        late + middle + early[::-1],
        2,
        (q_all, acc, top, total),
        jax.ShapeDtypeStruct((n, width), queries.dtype),
        [
            pltpu.VMEM(sums.shape, jnp.float32),
            pltpu.VMEM(tops.shape, jnp.float32),
            pltpu.VMEM(totals.shape, jnp.float32),
            pltpu.VMEM((n, width), queries.dtype),
            pltpu.SemaphoreType.DMA((groups,)),
        ],
        final=True,
    )
    return attended.reshape(1, n, width)


def solution(mesh):
    return jax.shard_map(
        body,
        mesh=mesh,
        in_specs=(
            P("dp", "ctx", None),
            P("dp", "ctx", None),
            P("dp", "ctx"),
            P("dp", "ctx"),
            P("dp", None),
        ),
        out_specs=P("dp", "ctx", None),
        check_vma=False,
    )
```

```python
import functools
import typing

import jax
import jax.numpy as jnp
from jax import lax
from jax.experimental import pallas as pl
from jax.experimental.pallas import tpu as pltpu
from jax.sharding import PartitionSpec as P


LOG2E = 1.4426950408889634
LOW = -1e30


def slots_of(labels, owners, capacity):
    n = labels.shape[1]
    hot = lax.broadcasted_iota(jnp.int32, (owners, n), 0) == labels
    hot16 = jnp.where(hot, 1.0, 0.0).astype(jnp.bfloat16)
    earlier = lax.broadcasted_iota(jnp.int32, (n, n), 0) < lax.broadcasted_iota(
        jnp.int32, (n, n), 1
    )
    earlier16 = jnp.where(earlier, 1.0, 0.0).astype(jnp.bfloat16)
    before = jnp.dot(hot16, earlier16, preferred_element_type=jnp.float32)
    rank = jnp.sum(jnp.where(hot, before, 0.0), axis=0, keepdims=True)
    return labels * capacity + rank.astype(jnp.int32)


def pack_kernel(owners, capacity, dest_hbm, rows_hbm, out_hbm, dest, rows, packed, sems):
    slots = owners * capacity
    n = rows.shape[0]
    fetch_dest = pltpu.make_async_copy(dest_hbm, dest, sems.at[0])
    fetch_rows = pltpu.make_async_copy(rows_hbm, rows, sems.at[1])
    fetch_dest.start()
    fetch_rows.start()
    fetch_dest.wait()
    slot = slots_of(dest[...], owners, capacity)
    half = slots // 2
    hot = [
        half * i + lax.broadcasted_iota(jnp.int32, (half, n), 0) == slot for i in range(2)
    ]
    picks = [jnp.where(h, 1.0, 0.0).astype(jnp.bfloat16) for h in hot]
    fetch_rows.wait()
    puts = []
    for i in range(2):
        part = pl.ds(half * i, half)
        packed[part, :] = jnp.dot(
            picks[i], rows[...], preferred_element_type=jnp.float32
        ).astype(packed.dtype)
        puts.append(
            pltpu.make_async_copy(packed.at[part, :], out_hbm.at[part, :], sems.at[2 + i])
        )
        puts[i].start()
    for put in puts:
        put.wait()


def picks_of(source_ref, owners, capacity):
    slots = slots_of(source_ref[...], owners, capacity)
    n = slots.shape[1]
    wide = jnp.broadcast_to(slots.astype(jnp.float32), (128, n))
    tall = jnp.transpose(wide).astype(jnp.int32)
    lane = lax.broadcasted_iota(jnp.int32, (n, 128), 1)
    parts = [
        jnp.where(tall == lane + 128 * i, 1.0, 0.0).astype(jnp.bfloat16)
        for i in range(owners * capacity // 128)
    ]
    return jnp.concatenate(parts, axis=1)


def picks_kernel(owners, capacity, source_ref, out_ref):
    out_ref[...] = picks_of(source_ref, owners, capacity)


def unpack_kernel(picks_ref, rows_ref, out_ref):
    out_ref[...] = jnp.dot(
        picks_ref[...], rows_ref[...], preferred_element_type=jnp.float32
    ).astype(out_ref.dtype)


def join_kernel(own_ref, other_ref, out_ref):
    n = own_ref.shape[0]
    core = lax.rem(lax.axis_index("ctx"), 2)
    out_ref[pl.ds(pl.multiple_of(core * n, n), n), :] = own_ref[...]
    out_ref[pl.ds(pl.multiple_of((1 - core) * n, n), n), :] = other_ref[...]


def split_query(head, picks, got_ref, q_all):
    groups = got_ref.shape[1] // head
    for h in range(0, groups, 2):
        both = jnp.dot(
            picks, got_ref[:, h * head : (h + 2) * head], preferred_element_type=jnp.float32
        ) * (LOG2E * head ** (-0.5))
        for i in range(2):
            exact = both[:, i * head : (i + 1) * head]
            high = exact.astype(q_all.dtype)
            at = 2 * (h + i) * head
            q_all[:, at : at + head] = high
            q_all[:, at + head : at + 2 * head] = (exact - high.astype(jnp.float32)).astype(
                q_all.dtype
            )


class Block(typing.NamedTuple):
    core: jax.Array
    own: jax.Array
    place: typing.Callable
    here: typing.Callable
    clear: typing.Callable
    late: typing.Callable
    step: typing.Callable


def block_of(head, far, lengths_ref, kv, q_all, acc, top, total):
    n = q_all.shape[0]
    groups = acc.shape[0]
    chunk = 2 * n
    me = lax.axis_index("ctx")
    chip = me // 2
    core = me - 2 * chip

    starts = [jnp.int32(0)]
    for i in range(lengths_ref.shape[1] - 1):
        starts.append(starts[-1] + lengths_ref[0, i])

    def start_of(position):
        found = jnp.zeros_like(position)
        for s in starts[1:]:
            found = jnp.where(position >= s, jnp.maximum(found, s), found)
        return found

    q_first = me * n
    q_pos = q_first + lax.broadcasted_iota(jnp.int32, (1, n), 1)
    q_start = start_of(q_pos)
    low = start_of(q_first)
    high = start_of(q_first + n - 1)

    def place(i):
        return (chip - jnp.where(core == 0, far[i][0], far[i][1])) * chunk

    def here(at):
        return (at >= 0) & (at + chunk > low)

    def clear(at):
        return (at >= high) & (at + chunk <= q_first)

    def late(at):
        return low >= at + n

    def tree_max(s):
        while s.shape[0] > 8:
            half = s.shape[0] // 2
            s = jnp.maximum(s[:half], s[half:])
        return jnp.max(s, axis=0, keepdims=True)

    def fold(w):
        return jnp.sum(w.reshape(-1, 8, w.shape[1]), axis=0)

    def step(row, rows, position, masked, mode):
        row = pl.multiple_of(row, n)
        keys = jnp.concatenate([kv[pl.ds(row, rows), :head]] * 2, axis=1)
        values = jnp.transpose(kv[pl.ds(row, rows), head:])
        if masked:
            k_pos = position + lax.broadcasted_iota(jnp.int32, (rows, n), 0)
            visible = (k_pos <= q_pos) & (k_pos >= q_start)

        def scores(h):
            s = lax.dot_general(
                keys,
                q_all[:, 2 * h * head : 2 * (h + 1) * head],
                (((1,), (1,)), ((), ())),
                preferred_element_type=jnp.float32,
            )
            return jnp.where(visible, s, LOW) if masked else s

        def weigh(h, s):
            fade = None
            if mode == "fixed":
                m = top[h]
            elif mode == "first":
                m = tree_max(s)
                top[h] = m
            else:
                old = top[h]
                m = jnp.maximum(old, tree_max(s))
                top[h] = m
                fade = jnp.exp2(old - m)
            w = jnp.exp2(s - m)
            if mode == "fixed":
                total[h] += fold(w)
            elif mode == "first":
                total[h] = fold(w)
            else:
                total[h] = total[h] * fade + fold(w)
            return w.astype(kv.dtype), fade

        def gather(h, w, fade):
            part = jnp.dot(values, w, preferred_element_type=jnp.float32)
            if mode == "fixed":
                acc[h] += part
            elif mode == "first":
                acc[h] = part
            else:
                acc[h] = acc[h] * fade + part

        lag = 2
        s_of, w_of = {}, {}
        for t in range(groups + 1 + lag):
            if t < groups:
                s_of[t] = scores(t)
            if 0 <= t - 1 < groups:
                w_of[t - 1] = weigh(t - 1, s_of.pop(t - 1))
            if 0 <= t - 1 - lag < groups:
                gather(t - 1 - lag, *w_of.pop(t - 1 - lag))

    return Block(core, chip * chunk, place, here, clear, late, step)


def part_kernel(head, far, first, final, *refs):
    lengths_ref = refs[0]
    if first:
        picks_ref, got_ref = refs[1:3]
        near = refs[3 : 3 + len(far)]
        q_all, acc, top, total, kv = refs[3 + len(far) :]
        split_query(head, picks_ref[...], got_ref, q_all)
    else:
        q_all, acc_ref, top_ref, total_ref = refs[1:5]
        near = refs[5 : 5 + len(far)]
        if final:
            out_ref, kv, acc, top, total, done, sems = refs[5 + len(far) :]
            top[...] = top_ref[...]
        else:
            acc, total, kv = refs[5 + len(far) :]
            top = top_ref
        acc[...] = acc_ref[...]
        total[...] = total_ref[...]
    n = q_all.shape[0]
    groups = acc.shape[0]
    chunk = 2 * n
    block = block_of(head, far, lengths_ref, kv, q_all, acc, top, total)

    def place(i, count):
        at = block.place(0)
        for j in range(1, count):
            at = jnp.where(i == j, block.place(j), at)
        return at

    skip = 1 if first else 0
    fresh = kv.shape[0] // chunk
    names = far[:fresh]
    for i in range(len(names)):

        @pl.when(block.here(block.place(i)))
        def _():
            kv[i * chunk : (i + 1) * chunk] = near[i][...]

    if first:

        @pl.when(block.core == 0)
        def _():
            block.step(0, n, block.own, True, "first")

        @pl.when(block.core != 0)
        def _():
            block.step(0, chunk, block.own, True, "first")

    @pl.loop(skip, len(names))
    def _(i):
        at = place(i, len(names))
        is_here = block.here(at)
        is_clear = block.clear(at)
        is_late = block.late(at)

        @pl.when(is_here & is_clear)
        def _():
            block.step(i * chunk, chunk, at, False, "fixed")

        @pl.when(is_here & jnp.logical_not(is_clear) & is_late)
        def _():
            block.step(i * chunk + n, n, at + n, True, "fixed")

        @pl.when(is_here & jnp.logical_not(is_clear | is_late))
        def _():
            block.step(i * chunk, chunk, at, True, "fixed")

    if not final:
        return

    most = total[0]
    for h in range(1, groups):
        most = jnp.maximum(most, total[h])

    @pl.when(jnp.max(most) > 2.0**64)
    def _():
        for h in range(groups):
            top[h] = jnp.full((1, n), LOW, jnp.float32)
            total[h] = jnp.zeros(total.shape[1:], jnp.float32)
            acc[h] = jnp.zeros(acc.shape[1:], jnp.float32)

        @pl.loop(0, len(far))
        def _(t):
            i = len(far) - 1 - t
            at = place(i, len(far))
            for j, ref in enumerate(near):

                @pl.when(i == j)
                def _():
                    kv[0:chunk] = ref[...]

            @pl.when(block.here(at))
            def _():
                block.step(0, chunk, at, True, "running")

    copies = []
    for h in range(groups):
        columns = pl.ds(h * head, head)
        share = 1.0 / jnp.sum(total[h], axis=0, keepdims=True)
        done[:, columns] = jnp.transpose((acc[h] * share).astype(done.dtype))
        copies.append(
            pltpu.make_async_copy(done.at[:, columns], out_ref.at[:, columns], sems.at[h])
        )
        copies[-1].start()
    for copy in copies:
        copy.wait()


def vmem(count):
    return [pl.BlockSpec(memory_space=pltpu.VMEM)] * count


def body(queries, keyvals, dest_bin, source_owner, seq_lengths):
    owners = lax.axis_size("dp")
    n_ctx = lax.axis_size("ctx")
    n = queries.shape[1]
    width = queries.shape[2]
    kv_width = keyvals.shape[2]
    head = kv_width // 2
    capacity = 2 * n // owners
    slots = owners * capacity

    def pack(rows):
        return pl.pallas_call(
            functools.partial(pack_kernel, owners, capacity),
            out_shape=jax.ShapeDtypeStruct((slots, rows.shape[1]), rows.dtype),
            in_specs=[pl.BlockSpec(memory_space=pl.ANY)] * 2,
            out_specs=pl.BlockSpec(memory_space=pl.ANY),
            scratch_shapes=[
                pltpu.VMEM(dest_bin.shape, dest_bin.dtype),
                pltpu.VMEM(rows.shape, rows.dtype),
                pltpu.VMEM((slots, rows.shape[1]), rows.dtype),
                pltpu.SemaphoreType.DMA((4,)),
            ],
            cost_estimate=pl.CostEstimate(
                flops=2 * slots * n * rows.shape[1],
                bytes_accessed=6 * n * rows.shape[1],
                transcendentals=0,
            ),
        )(dest_bin, rows)

    def exchange(rows):
        return lax.all_to_all(
            rows.reshape(owners, capacity, rows.shape[1]),
            "dp",
            split_axis=0,
            concat_axis=0,
            tiled=True,
        ).reshape(slots, rows.shape[1])

    got_kv = exchange(pack(keyvals[0]))
    got_q = exchange(pack(queries[0]))
    picks = pl.pallas_call(
        functools.partial(picks_kernel, owners, capacity),
        out_shape=jax.ShapeDtypeStruct((n, slots), keyvals.dtype),
        in_specs=vmem(1),
        out_specs=vmem(1)[0],
        compiler_params=pltpu.CompilerParams(vmem_limit_bytes=4 << 20),
        cost_estimate=pl.CostEstimate(
            flops=2 * n * n * owners, bytes_accessed=2 * n * slots, transcendentals=0
        ),
    )(source_owner)
    own = pl.pallas_call(
        unpack_kernel,
        out_shape=jax.ShapeDtypeStruct((n, kv_width), keyvals.dtype),
        in_specs=vmem(2),
        out_specs=vmem(1)[0],
        compiler_params=pltpu.CompilerParams(vmem_limit_bytes=12 << 20),
        cost_estimate=pl.CostEstimate(
            flops=2 * slots * n * kv_width,
            bytes_accessed=6 * n * kv_width,
            transcendentals=0,
        ),
    )(picks, got_kv)

    def hop(x, up, down):
        return lax.ppermute(
            x,
            "ctx",
            [(c, (c + (2 * up if c % 2 == 0 else -2 * down)) % n_ctx) for c in range(n_ctx)],
        )

    def swap(x):
        return lax.ppermute(x, "ctx", [(c, c ^ 1) for c in range(n_ctx)])

    other = swap(own)
    pair = pl.pallas_call(
        join_kernel,
        out_shape=jax.ShapeDtypeStruct((2 * n, kv_width), keyvals.dtype),
        in_specs=vmem(2),
        out_specs=vmem(1)[0],
        compiler_params=pltpu.CompilerParams(vmem_limit_bytes=4 << 20),
        cost_estimate=pl.CostEstimate(
            flops=0, bytes_accessed=8 * n * kv_width, transcendentals=0
        ),
    )(own, other)
    hop1 = hop(pair, 1, 2)
    hop2 = hop(hop1, 1, 1)
    hop3 = hop(hop1, 2, 2)
    groups = width // head
    query = jax.ShapeDtypeStruct((n, 2 * width), queries.dtype)
    sums = jax.ShapeDtypeStruct((groups, head, n), jnp.float32)
    tops = jax.ShapeDtypeStruct((groups, 1, n), jnp.float32)
    totals = jax.ShapeDtypeStruct((groups, 8, n), jnp.float32)

    def attend(pieces, fresh, inputs, outputs, scratch, first=False, final=False):
        return pl.pallas_call(
            functools.partial(part_kernel, head, [f for f, _ in pieces], first, final),
            out_shape=outputs,
            in_specs=[pl.BlockSpec(memory_space=pltpu.SMEM)] + vmem(len(inputs) + len(pieces)),
            out_specs=pl.BlockSpec(memory_space=pl.ANY) if final else tuple(vmem(len(outputs))),
            scratch_shapes=[pltpu.VMEM((2 * n * fresh, kv_width), keyvals.dtype)] + scratch,
            compiler_params=pltpu.CompilerParams(vmem_limit_bytes=20 << 20),
            cost_estimate=pl.CostEstimate(
                flops=8 * n * n * width * fresh,
                bytes_accessed=8 * n * width,
                transcendentals=2 * n * n * groups * fresh,
            ),
        )(seq_lengths, *inputs, *[x for _, x in pieces])

    swapped1 = swap(hop1)
    early = [((0, 0), pair), ((1, 6), hop1), ((6, 1), swapped1)]
    swapped2 = swap(hop2)
    swapped3 = swap(hop3)
    middle = [((2, 5), hop2), ((5, 2), swapped2)]
    late = [((3, 4), hop3), ((4, 3), swapped3)]
    q_all, acc, top, total = attend(
        early, 3, (picks, got_q), (query, sums, tops, totals), [], first=True
    )
    acc, total = attend(middle, 2, (q_all, acc, top, total), (sums, totals), [])
    attended = attend(
        late + middle + early[::-1],
        2,
        (q_all, acc, top, total),
        jax.ShapeDtypeStruct((n, width), queries.dtype),
        [
            pltpu.VMEM(sums.shape, jnp.float32),
            pltpu.VMEM(tops.shape, jnp.float32),
            pltpu.VMEM(totals.shape, jnp.float32),
            pltpu.VMEM((n, width), queries.dtype),
            pltpu.SemaphoreType.DMA((groups,)),
        ],
        final=True,
    )
    return attended.reshape(1, n, width)


def solution(mesh):
    return jax.shard_map(
        body,
        mesh=mesh,
        in_specs=(
            P("dp", "ctx", None),
            P("dp", "ctx", None),
            P("dp", "ctx"),
            P("dp", "ctx"),
            P("dp", None),
        ),
        out_specs=P("dp", "ctx", None),
        check_vma=False,
    )
```

```python
import functools
import typing

import jax
import jax.numpy as jnp
from jax import lax
from jax.experimental import pallas as pl
from jax.experimental.pallas import tpu as pltpu
from jax.sharding import PartitionSpec as P


LOG2E = 1.4426950408889634
LOW = -1e30


def slots_of(labels, owners, capacity):
    n = labels.shape[1]
    hot = lax.broadcasted_iota(jnp.int32, (owners, n), 0) == labels
    hot16 = jnp.where(hot, 1.0, 0.0).astype(jnp.bfloat16)
    earlier = lax.broadcasted_iota(jnp.int32, (n, n), 0) < lax.broadcasted_iota(
        jnp.int32, (n, n), 1
    )
    earlier16 = jnp.where(earlier, 1.0, 0.0).astype(jnp.bfloat16)
    before = jnp.dot(hot16, earlier16, preferred_element_type=jnp.float32)
    rank = jnp.sum(jnp.where(hot, before, 0.0), axis=0, keepdims=True)
    return labels * capacity + rank.astype(jnp.int32)


def pack_kernel(owners, capacity, dest_hbm, rows_hbm, out_hbm, dest, rows, packed, sems):
    slots = owners * capacity
    n = rows.shape[0]
    fetch_dest = pltpu.make_async_copy(dest_hbm, dest, sems.at[0])
    fetch_rows = pltpu.make_async_copy(rows_hbm, rows, sems.at[1])
    fetch_dest.start()
    fetch_rows.start()
    fetch_dest.wait()
    slot = slots_of(dest[...], owners, capacity)
    half = slots // 2
    hot = [
        half * i + lax.broadcasted_iota(jnp.int32, (half, n), 0) == slot for i in range(2)
    ]
    picks = [jnp.where(h, 1.0, 0.0).astype(jnp.bfloat16) for h in hot]
    fetch_rows.wait()
    puts = []
    for i in range(2):
        part = pl.ds(half * i, half)
        packed[part, :] = jnp.dot(
            picks[i], rows[...], preferred_element_type=jnp.float32
        ).astype(packed.dtype)
        puts.append(
            pltpu.make_async_copy(packed.at[part, :], out_hbm.at[part, :], sems.at[2 + i])
        )
        puts[i].start()
    for put in puts:
        put.wait()


def picks_of(source_ref, owners, capacity):
    slots = slots_of(source_ref[...], owners, capacity)
    n = slots.shape[1]
    wide = jnp.broadcast_to(slots.astype(jnp.float32), (128, n))
    tall = jnp.transpose(wide).astype(jnp.int32)
    lane = lax.broadcasted_iota(jnp.int32, (n, 128), 1)
    parts = [
        jnp.where(tall == lane + 128 * i, 1.0, 0.0).astype(jnp.bfloat16)
        for i in range(owners * capacity // 128)
    ]
    return jnp.concatenate(parts, axis=1)


def picks_kernel(owners, capacity, source_ref, out_ref):
    out_ref[...] = picks_of(source_ref, owners, capacity)


def unpack_kernel(picks_ref, rows_ref, out_ref):
    out_ref[...] = jnp.dot(
        picks_ref[...], rows_ref[...], preferred_element_type=jnp.float32
    ).astype(out_ref.dtype)


def join_kernel(own_ref, other_ref, out_ref):
    n = own_ref.shape[0]
    core = lax.rem(lax.axis_index("ctx"), 2)
    out_ref[pl.ds(pl.multiple_of(core * n, n), n), :] = own_ref[...]
    out_ref[pl.ds(pl.multiple_of((1 - core) * n, n), n), :] = other_ref[...]


def split_query(head, picks, got_ref, q_all):
    groups = got_ref.shape[1] // head
    for h in range(0, groups, 2):
        both = jnp.dot(
            picks, got_ref[:, h * head : (h + 2) * head], preferred_element_type=jnp.float32
        ) * (LOG2E * head ** (-0.5))
        for i in range(2):
            exact = both[:, i * head : (i + 1) * head]
            high = exact.astype(q_all.dtype)
            at = 2 * (h + i) * head
            q_all[:, at : at + head] = high
            q_all[:, at + head : at + 2 * head] = (exact - high.astype(jnp.float32)).astype(
                q_all.dtype
            )


class Block(typing.NamedTuple):
    core: jax.Array
    own: jax.Array
    place: typing.Callable
    here: typing.Callable
    clear: typing.Callable
    late: typing.Callable
    step: typing.Callable


def block_of(head, far, lengths_ref, kv, q_all, acc, top, total):
    n = q_all.shape[0]
    groups = acc.shape[0]
    chunk = 2 * n
    me = lax.axis_index("ctx")
    chip = me // 2
    core = me - 2 * chip

    starts = [jnp.int32(0)]
    for i in range(lengths_ref.shape[1] - 1):
        starts.append(starts[-1] + lengths_ref[0, i])

    def start_of(position):
        found = jnp.zeros_like(position)
        for s in starts[1:]:
            found = jnp.where(position >= s, jnp.maximum(found, s), found)
        return found

    q_first = me * n
    q_pos = q_first + lax.broadcasted_iota(jnp.int32, (1, n), 1)
    q_start = start_of(q_pos)
    low = start_of(q_first)
    high = start_of(q_first + n - 1)

    def place(i):
        return (chip - jnp.where(core == 0, far[i][0], far[i][1])) * chunk

    def here(at):
        return (at >= 0) & (at + chunk > low)

    def clear(at):
        return (at >= high) & (at + chunk <= q_first)

    def late(at):
        return low >= at + n

    def tree_max(s):
        while s.shape[0] > 8:
            half = s.shape[0] // 2
            s = jnp.maximum(s[:half], s[half:])
        return jnp.max(s, axis=0, keepdims=True)

    def fold(w):
        return jnp.sum(w.reshape(-1, 8, w.shape[1]), axis=0)

    def step(row, rows, position, masked, mode):
        row = pl.multiple_of(row, n)
        keys = jnp.concatenate([kv[pl.ds(row, rows), :head]] * 2, axis=1)
        values = jnp.transpose(kv[pl.ds(row, rows), head:])
        if masked:
            k_pos = position + lax.broadcasted_iota(jnp.int32, (rows, n), 0)
            visible = (k_pos <= q_pos) & (k_pos >= q_start)

        def scores(h):
            s = lax.dot_general(
                keys,
                q_all[:, 2 * h * head : 2 * (h + 1) * head],
                (((1,), (1,)), ((), ())),
                preferred_element_type=jnp.float32,
            )
            return jnp.where(visible, s, LOW) if masked else s

        def weigh(h, s):
            fade = None
            if mode == "fixed":
                m = top[h]
            elif mode == "first":
                m = tree_max(s)
                top[h] = m
            else:
                old = top[h]
                m = jnp.maximum(old, tree_max(s))
                top[h] = m
                fade = jnp.exp2(old - m)
            w = jnp.exp2(s - m)
            if mode == "fixed":
                total[h] += fold(w)
            elif mode == "first":
                total[h] = fold(w)
            else:
                total[h] = total[h] * fade + fold(w)
            return w.astype(kv.dtype), fade

        def gather(h, w, fade):
            part = jnp.dot(values, w, preferred_element_type=jnp.float32)
            if mode == "fixed":
                acc[h] += part
            elif mode == "first":
                acc[h] = part
            else:
                acc[h] = acc[h] * fade + part

        lag = 2
        s_of, w_of = {}, {}
        for t in range(groups + 1 + lag):
            if t < groups:
                s_of[t] = scores(t)
            if 0 <= t - 1 < groups:
                w_of[t - 1] = weigh(t - 1, s_of.pop(t - 1))
            if 0 <= t - 1 - lag < groups:
                gather(t - 1 - lag, *w_of.pop(t - 1 - lag))

    return Block(core, chip * chunk, place, here, clear, late, step)


def part_kernel(head, far, first, final, *refs):
    lengths_ref = refs[0]
    if first:
        picks_ref, got_ref = refs[1:3]
        near = refs[3 : 3 + len(far)]
        q_all, acc, top, total, kv = refs[3 + len(far) :]
        split_query(head, picks_ref[...], got_ref, q_all)
    else:
        q_all, acc_ref, top_ref, total_ref = refs[1:5]
        near = refs[5 : 5 + len(far)]
        if final:
            out_ref, kv, acc, top, total, done, sems = refs[5 + len(far) :]
            top[...] = top_ref[...]
        else:
            acc, total, kv = refs[5 + len(far) :]
            top = top_ref
        acc[...] = acc_ref[...]
        total[...] = total_ref[...]
    n = q_all.shape[0]
    groups = acc.shape[0]
    chunk = 2 * n
    block = block_of(head, far, lengths_ref, kv, q_all, acc, top, total)

    def place(i, count):
        at = block.place(0)
        for j in range(1, count):
            at = jnp.where(i == j, block.place(j), at)
        return at

    skip = 1 if first else 0
    fresh = kv.shape[0] // chunk
    names = far[:fresh]
    for i in range(len(names)):

        @pl.when(block.here(block.place(i)))
        def _():
            kv[i * chunk : (i + 1) * chunk] = near[i][...]

    if first:

        @pl.when(block.core == 0)
        def _():
            block.step(0, n, block.own, True, "first")

        @pl.when(block.core != 0)
        def _():
            block.step(0, chunk, block.own, True, "first")

    @pl.loop(skip, len(names))
    def _(i):
        at = place(i, len(names))
        is_here = block.here(at)
        is_clear = block.clear(at)
        is_late = block.late(at)

        @pl.when(is_here & is_clear)
        def _():
            block.step(i * chunk, chunk, at, False, "fixed")

        @pl.when(is_here & jnp.logical_not(is_clear) & is_late)
        def _():
            block.step(i * chunk + n, n, at + n, True, "fixed")

        @pl.when(is_here & jnp.logical_not(is_clear | is_late))
        def _():
            block.step(i * chunk, chunk, at, True, "fixed")

    if not final:
        return

    most = total[0]
    for h in range(1, groups):
        most = jnp.maximum(most, total[h])

    @pl.when(jnp.max(most) > 2.0**64)
    def _():
        for h in range(groups):
            top[h] = jnp.full((1, n), LOW, jnp.float32)
            total[h] = jnp.zeros(total.shape[1:], jnp.float32)
            acc[h] = jnp.zeros(acc.shape[1:], jnp.float32)

        @pl.loop(0, len(far))
        def _(t):
            i = len(far) - 1 - t
            at = place(i, len(far))
            for j, ref in enumerate(near):

                @pl.when(i == j)
                def _():
                    kv[0:chunk] = ref[...]

            @pl.when(block.here(at))
            def _():
                block.step(0, chunk, at, True, "running")

    copies = []
    for h in range(groups):
        columns = pl.ds(h * head, head)
        share = 1.0 / jnp.sum(total[h], axis=0, keepdims=True)
        done[:, columns] = jnp.transpose((acc[h] * share).astype(done.dtype))
        copies.append(
            pltpu.make_async_copy(done.at[:, columns], out_ref.at[:, columns], sems.at[h])
        )
        copies[-1].start()
    for copy in copies:
        copy.wait()


def vmem(count):
    return [pl.BlockSpec(memory_space=pltpu.VMEM)] * count


def body(queries, keyvals, dest_bin, source_owner, seq_lengths):
    owners = lax.axis_size("dp")
    n_ctx = lax.axis_size("ctx")
    n = queries.shape[1]
    width = queries.shape[2]
    kv_width = keyvals.shape[2]
    head = kv_width // 2
    capacity = 2 * n // owners
    slots = owners * capacity

    def pack(rows):
        return pl.pallas_call(
            functools.partial(pack_kernel, owners, capacity),
            out_shape=jax.ShapeDtypeStruct((slots, rows.shape[1]), rows.dtype),
            in_specs=[pl.BlockSpec(memory_space=pl.ANY)] * 2,
            out_specs=pl.BlockSpec(memory_space=pl.ANY),
            scratch_shapes=[
                pltpu.VMEM(dest_bin.shape, dest_bin.dtype),
                pltpu.VMEM(rows.shape, rows.dtype),
                pltpu.VMEM((slots, rows.shape[1]), rows.dtype),
                pltpu.SemaphoreType.DMA((4,)),
            ],
            cost_estimate=pl.CostEstimate(
                flops=2 * slots * n * rows.shape[1],
                bytes_accessed=6 * n * rows.shape[1],
                transcendentals=0,
            ),
        )(dest_bin, rows)

    def exchange(rows):
        return lax.all_to_all(
            rows.reshape(owners, capacity, rows.shape[1]),
            "dp",
            split_axis=0,
            concat_axis=0,
            tiled=True,
        ).reshape(slots, rows.shape[1])

    got_kv = exchange(pack(keyvals[0]))
    got_q = exchange(pack(queries[0]))
    picks = pl.pallas_call(
        functools.partial(picks_kernel, owners, capacity),
        out_shape=jax.ShapeDtypeStruct((n, slots), keyvals.dtype),
        in_specs=vmem(1),
        out_specs=vmem(1)[0],
        compiler_params=pltpu.CompilerParams(vmem_limit_bytes=4 << 20),
        cost_estimate=pl.CostEstimate(
            flops=2 * n * n * owners, bytes_accessed=2 * n * slots, transcendentals=0
        ),
    )(source_owner)
    own = pl.pallas_call(
        unpack_kernel,
        out_shape=jax.ShapeDtypeStruct((n, kv_width), keyvals.dtype),
        in_specs=vmem(2),
        out_specs=vmem(1)[0],
        compiler_params=pltpu.CompilerParams(vmem_limit_bytes=12 << 20),
        cost_estimate=pl.CostEstimate(
            flops=2 * slots * n * kv_width,
            bytes_accessed=6 * n * kv_width,
            transcendentals=0,
        ),
    )(picks, got_kv)

    def hop(x, up, down):
        return lax.ppermute(
            x,
            "ctx",
            [(c, (c + (2 * up if c % 2 == 0 else -2 * down)) % n_ctx) for c in range(n_ctx)],
        )

    def swap(x):
        return lax.ppermute(x, "ctx", [(c, c ^ 1) for c in range(n_ctx)])

    other = swap(own)
    pair = pl.pallas_call(
        join_kernel,
        out_shape=jax.ShapeDtypeStruct((2 * n, kv_width), keyvals.dtype),
        in_specs=vmem(2),
        out_specs=vmem(1)[0],
        compiler_params=pltpu.CompilerParams(vmem_limit_bytes=4 << 20),
        cost_estimate=pl.CostEstimate(
            flops=0, bytes_accessed=8 * n * kv_width, transcendentals=0
        ),
    )(own, other)
    hop1 = hop(pair, 1, 2)
    hop2 = hop(hop1, 1, 1)
    hop3 = hop(hop1, 2, 2)
    groups = width // head
    query = jax.ShapeDtypeStruct((n, 2 * width), queries.dtype)
    sums = jax.ShapeDtypeStruct((groups, head, n), jnp.float32)
    tops = jax.ShapeDtypeStruct((groups, 1, n), jnp.float32)
    totals = jax.ShapeDtypeStruct((groups, 8, n), jnp.float32)

    def attend(pieces, fresh, inputs, outputs, scratch, first=False, final=False):
        return pl.pallas_call(
            functools.partial(part_kernel, head, [f for f, _ in pieces], first, final),
            out_shape=outputs,
            in_specs=[pl.BlockSpec(memory_space=pltpu.SMEM)] + vmem(len(inputs) + len(pieces)),
            out_specs=pl.BlockSpec(memory_space=pl.ANY) if final else tuple(vmem(len(outputs))),
            scratch_shapes=[pltpu.VMEM((2 * n * fresh, kv_width), keyvals.dtype)] + scratch,
            compiler_params=pltpu.CompilerParams(vmem_limit_bytes=20 << 20),
            cost_estimate=pl.CostEstimate(
                flops=8 * n * n * width * fresh,
                bytes_accessed=8 * n * width,
                transcendentals=2 * n * n * groups * fresh,
            ),
        )(seq_lengths, *inputs, *[x for _, x in pieces])

    swapped1 = swap(hop1)
    early = [((0, 0), pair), ((1, 6), hop1), ((6, 1), swapped1)]
    swapped2 = swap(hop2)
    swapped3 = swap(hop3)
    middle = [((2, 5), hop2)]
    later = [((5, 2), swapped2), ((3, 4), hop3)]
    last = [((4, 3), swapped3)]
    q_all, acc, top, total = attend(
        early, 3, (picks, got_q), (query, sums, tops, totals), [], first=True
    )
    acc, total = attend(middle, 1, (q_all, acc, top, total), (sums, totals), [])
    acc, total = attend(later, 2, (q_all, acc, top, total), (sums, totals), [])
    attended = attend(
        last + later + middle + early[::-1],
        1,
        (q_all, acc, top, total),
        jax.ShapeDtypeStruct((n, width), queries.dtype),
        [
            pltpu.VMEM(sums.shape, jnp.float32),
            pltpu.VMEM(tops.shape, jnp.float32),
            pltpu.VMEM(totals.shape, jnp.float32),
            pltpu.VMEM((n, width), queries.dtype),
            pltpu.SemaphoreType.DMA((groups,)),
        ],
        final=True,
    )
    return attended.reshape(1, n, width)


def solution(mesh):
    return jax.shard_map(
        body,
        mesh=mesh,
        in_specs=(
            P("dp", "ctx", None),
            P("dp", "ctx", None),
            P("dp", "ctx"),
            P("dp", "ctx"),
            P("dp", None),
        ),
        out_specs=P("dp", "ctx", None),
        check_vma=False,
    )
```

```python
import functools
import typing

import jax
import jax.numpy as jnp
from jax import lax
from jax.experimental import pallas as pl
from jax.experimental.pallas import tpu as pltpu
from jax.sharding import PartitionSpec as P


LOG2E = 1.4426950408889634
LOW = -1e30


def slots_of(labels, owners, capacity):
    n = labels.shape[1]
    hot = lax.broadcasted_iota(jnp.int32, (owners, n), 0) == labels
    hot16 = jnp.where(hot, 1.0, 0.0).astype(jnp.bfloat16)
    earlier = lax.broadcasted_iota(jnp.int32, (n, n), 0) < lax.broadcasted_iota(
        jnp.int32, (n, n), 1
    )
    earlier16 = jnp.where(earlier, 1.0, 0.0).astype(jnp.bfloat16)
    before = jnp.dot(hot16, earlier16, preferred_element_type=jnp.float32)
    rank = jnp.sum(jnp.where(hot, before, 0.0), axis=0, keepdims=True)
    return labels * capacity + rank.astype(jnp.int32)


def pack_kernel(owners, capacity, dest_hbm, rows_hbm, out_hbm, dest, rows, packed, sems):
    slots = owners * capacity
    n = rows.shape[0]
    fetch_dest = pltpu.make_async_copy(dest_hbm, dest, sems.at[0])
    fetch_rows = pltpu.make_async_copy(rows_hbm, rows, sems.at[1])
    fetch_dest.start()
    fetch_rows.start()
    fetch_dest.wait()
    slot = slots_of(dest[...], owners, capacity)
    half = slots // 2
    hot = [
        half * i + lax.broadcasted_iota(jnp.int32, (half, n), 0) == slot for i in range(2)
    ]
    picks = [jnp.where(h, 1.0, 0.0).astype(jnp.bfloat16) for h in hot]
    fetch_rows.wait()
    puts = []
    for i in range(2):
        part = pl.ds(half * i, half)
        packed[part, :] = jnp.dot(
            picks[i], rows[...], preferred_element_type=jnp.float32
        ).astype(packed.dtype)
        puts.append(
            pltpu.make_async_copy(packed.at[part, :], out_hbm.at[part, :], sems.at[2 + i])
        )
        puts[i].start()
    for put in puts:
        put.wait()


def picks_of(source_ref, owners, capacity):
    slots = slots_of(source_ref[...], owners, capacity)
    n = slots.shape[1]
    wide = jnp.broadcast_to(slots.astype(jnp.float32), (128, n))
    tall = jnp.transpose(wide).astype(jnp.int32)
    lane = lax.broadcasted_iota(jnp.int32, (n, 128), 1)
    parts = [
        jnp.where(tall == lane + 128 * i, 1.0, 0.0).astype(jnp.bfloat16)
        for i in range(owners * capacity // 128)
    ]
    return jnp.concatenate(parts, axis=1)


def picks_kernel(owners, capacity, source_ref, out_ref):
    out_ref[...] = picks_of(source_ref, owners, capacity)


def unpack_kernel(picks_ref, rows_ref, out_ref):
    out_ref[...] = jnp.dot(
        picks_ref[...], rows_ref[...], preferred_element_type=jnp.float32
    ).astype(out_ref.dtype)


def join_kernel(own_ref, other_ref, out_ref):
    n = own_ref.shape[0]
    core = lax.rem(lax.axis_index("ctx"), 2)
    out_ref[pl.ds(pl.multiple_of(core * n, n), n), :] = own_ref[...]
    out_ref[pl.ds(pl.multiple_of((1 - core) * n, n), n), :] = other_ref[...]


def split_query(head, picks, got_ref, q_all):
    groups = got_ref.shape[1] // head
    for h in range(0, groups, 2):
        both = jnp.dot(
            picks, got_ref[:, h * head : (h + 2) * head], preferred_element_type=jnp.float32
        ) * (LOG2E * head ** (-0.5))
        for i in range(2):
            exact = both[:, i * head : (i + 1) * head]
            high = exact.astype(q_all.dtype)
            at = 2 * (h + i) * head
            q_all[:, at : at + head] = high
            q_all[:, at + head : at + 2 * head] = (exact - high.astype(jnp.float32)).astype(
                q_all.dtype
            )


class Block(typing.NamedTuple):
    core: jax.Array
    own: jax.Array
    place: typing.Callable
    here: typing.Callable
    clear: typing.Callable
    late: typing.Callable
    step: typing.Callable


def block_of(head, far, lengths_ref, kv, q_all, acc, top, total):
    n = q_all.shape[0]
    groups = acc.shape[0]
    chunk = 2 * n
    me = lax.axis_index("ctx")
    chip = me // 2
    core = me - 2 * chip

    starts = [jnp.int32(0)]
    for i in range(lengths_ref.shape[1] - 1):
        starts.append(starts[-1] + lengths_ref[0, i])

    def start_of(position):
        found = jnp.zeros_like(position)
        for s in starts[1:]:
            found = jnp.where(position >= s, jnp.maximum(found, s), found)
        return found

    q_first = me * n
    q_pos = q_first + lax.broadcasted_iota(jnp.int32, (1, n), 1)
    q_start = start_of(q_pos)
    low = start_of(q_first)
    high = start_of(q_first + n - 1)

    def place(i):
        return (chip - jnp.where(core == 0, far[i][0], far[i][1])) * chunk

    def here(at):
        return (at >= 0) & (at + chunk > low)

    def clear(at):
        return (at >= high) & (at + chunk <= q_first)

    def late(at):
        return low >= at + n

    def tree_max(s):
        while s.shape[0] > 8:
            half = s.shape[0] // 2
            s = jnp.maximum(s[:half], s[half:])
        return jnp.max(s, axis=0, keepdims=True)

    def fold(w):
        return jnp.sum(w.reshape(-1, 8, w.shape[1]), axis=0)

    def step(row, rows, position, masked, mode):
        row = pl.multiple_of(row, n)
        keys = jnp.concatenate([kv[pl.ds(row, rows), :head]] * 2, axis=1)
        values = jnp.transpose(kv[pl.ds(row, rows), head:])
        if masked:
            k_pos = position + lax.broadcasted_iota(jnp.int32, (rows, n), 0)
            visible = (k_pos <= q_pos) & (k_pos >= q_start)

        def scores(h):
            s = lax.dot_general(
                keys,
                q_all[:, 2 * h * head : 2 * (h + 1) * head],
                (((1,), (1,)), ((), ())),
                preferred_element_type=jnp.float32,
            )
            return jnp.where(visible, s, LOW) if masked else s

        def weigh(h, s):
            fade = None
            if mode == "fixed":
                m = top[h]
            elif mode == "first":
                m = tree_max(s)
                top[h] = m
            else:
                old = top[h]
                m = jnp.maximum(old, tree_max(s))
                top[h] = m
                fade = jnp.exp2(old - m)
            w = jnp.exp2(s - m)
            if mode == "fixed":
                total[h] += fold(w)
            elif mode == "first":
                total[h] = fold(w)
            else:
                total[h] = total[h] * fade + fold(w)
            return w.astype(kv.dtype), fade

        def gather(h, w, fade):
            part = jnp.dot(values, w, preferred_element_type=jnp.float32)
            if mode == "fixed":
                acc[h] += part
            elif mode == "first":
                acc[h] = part
            else:
                acc[h] = acc[h] * fade + part

        lag = 2
        s_of, w_of = {}, {}
        for t in range(groups + 1 + lag):
            if t < groups:
                s_of[t] = scores(t)
            if 0 <= t - 1 < groups:
                w_of[t - 1] = weigh(t - 1, s_of.pop(t - 1))
            if 0 <= t - 1 - lag < groups:
                gather(t - 1 - lag, *w_of.pop(t - 1 - lag))

    return Block(core, chip * chunk, place, here, clear, late, step)


def part_kernel(head, far, first, final, *refs):
    lengths_ref = refs[0]
    if first:
        picks_ref, got_ref = refs[1:3]
        near = refs[3 : 3 + len(far)]
        q_all, acc, top, total, kv = refs[3 + len(far) :]
        split_query(head, picks_ref[...], got_ref, q_all)
    else:
        q_all, acc_ref, top_ref, total_ref = refs[1:5]
        near = refs[5 : 5 + len(far)]
        if final:
            out_ref, kv, acc, top, total, done, sems = refs[5 + len(far) :]
            top[...] = top_ref[...]
        else:
            acc, total, kv = refs[5 + len(far) :]
            top = top_ref
        acc[...] = acc_ref[...]
        total[...] = total_ref[...]
    n = q_all.shape[0]
    groups = acc.shape[0]
    chunk = 2 * n
    block = block_of(head, far, lengths_ref, kv, q_all, acc, top, total)

    def place(i, count):
        at = block.place(0)
        for j in range(1, count):
            at = jnp.where(i == j, block.place(j), at)
        return at

    skip = 1 if first else 0
    fresh = kv.shape[0] // chunk
    names = far[:fresh]
    for i in range(len(names)):

        @pl.when(block.here(block.place(i)))
        def _():
            kv[i * chunk : (i + 1) * chunk] = near[i][...]

    if first:

        @pl.when(block.core == 0)
        def _():
            block.step(0, n, block.own, True, "first")

        @pl.when(block.core != 0)
        def _():
            block.step(0, chunk, block.own, True, "first")

    def usable(i):
        at = block.place(i)
        return block.here(at) & block.clear(at)

    pair = jnp.bool_(False)
    if not first and len(names) == 2:
        pair = usable(0) & usable(1)

        @pl.when(pair)
        def _():
            block.step(0, 2 * chunk, 0, False, "fixed")

    @pl.loop(skip, len(names))
    def _(i):
        at = place(i, len(names))
        is_here = block.here(at) & jnp.logical_not(pair)
        is_clear = block.clear(at)
        is_late = block.late(at)

        @pl.when(is_here & is_clear)
        def _():
            block.step(i * chunk, chunk, at, False, "fixed")

        @pl.when(is_here & jnp.logical_not(is_clear) & is_late)
        def _():
            block.step(i * chunk + n, n, at + n, True, "fixed")

        @pl.when(is_here & jnp.logical_not(is_clear | is_late))
        def _():
            block.step(i * chunk, chunk, at, True, "fixed")

    if not final:
        return

    most = total[0]
    for h in range(1, groups):
        most = jnp.maximum(most, total[h])

    @pl.when(jnp.max(most) > 2.0**64)
    def _():
        for h in range(groups):
            top[h] = jnp.full((1, n), LOW, jnp.float32)
            total[h] = jnp.zeros(total.shape[1:], jnp.float32)
            acc[h] = jnp.zeros(acc.shape[1:], jnp.float32)

        @pl.loop(0, len(far))
        def _(t):
            i = len(far) - 1 - t
            at = place(i, len(far))
            for j, ref in enumerate(near):

                @pl.when(i == j)
                def _():
                    kv[0:chunk] = ref[...]

            @pl.when(block.here(at))
            def _():
                block.step(0, chunk, at, True, "running")

    copies = []
    for h in range(groups):
        columns = pl.ds(h * head, head)
        share = 1.0 / jnp.sum(total[h], axis=0, keepdims=True)
        done[:, columns] = jnp.transpose((acc[h] * share).astype(done.dtype))
        copies.append(
            pltpu.make_async_copy(done.at[:, columns], out_ref.at[:, columns], sems.at[h])
        )
        copies[-1].start()
    for copy in copies:
        copy.wait()


def vmem(count):
    return [pl.BlockSpec(memory_space=pltpu.VMEM)] * count


def body(queries, keyvals, dest_bin, source_owner, seq_lengths):
    owners = lax.axis_size("dp")
    n_ctx = lax.axis_size("ctx")
    n = queries.shape[1]
    width = queries.shape[2]
    kv_width = keyvals.shape[2]
    head = kv_width // 2
    capacity = 2 * n // owners
    slots = owners * capacity

    def pack(rows):
        return pl.pallas_call(
            functools.partial(pack_kernel, owners, capacity),
            out_shape=jax.ShapeDtypeStruct((slots, rows.shape[1]), rows.dtype),
            in_specs=[pl.BlockSpec(memory_space=pl.ANY)] * 2,
            out_specs=pl.BlockSpec(memory_space=pl.ANY),
            scratch_shapes=[
                pltpu.VMEM(dest_bin.shape, dest_bin.dtype),
                pltpu.VMEM(rows.shape, rows.dtype),
                pltpu.VMEM((slots, rows.shape[1]), rows.dtype),
                pltpu.SemaphoreType.DMA((4,)),
            ],
            cost_estimate=pl.CostEstimate(
                flops=2 * slots * n * rows.shape[1],
                bytes_accessed=6 * n * rows.shape[1],
                transcendentals=0,
            ),
        )(dest_bin, rows)

    def exchange(rows):
        return lax.all_to_all(
            rows.reshape(owners, capacity, rows.shape[1]),
            "dp",
            split_axis=0,
            concat_axis=0,
            tiled=True,
        ).reshape(slots, rows.shape[1])

    got_kv = exchange(pack(keyvals[0]))
    got_q = exchange(pack(queries[0]))
    picks = pl.pallas_call(
        functools.partial(picks_kernel, owners, capacity),
        out_shape=jax.ShapeDtypeStruct((n, slots), keyvals.dtype),
        in_specs=vmem(1),
        out_specs=vmem(1)[0],
        compiler_params=pltpu.CompilerParams(vmem_limit_bytes=4 << 20),
        cost_estimate=pl.CostEstimate(
            flops=2 * n * n * owners, bytes_accessed=2 * n * slots, transcendentals=0
        ),
    )(source_owner)
    own = pl.pallas_call(
        unpack_kernel,
        out_shape=jax.ShapeDtypeStruct((n, kv_width), keyvals.dtype),
        in_specs=vmem(2),
        out_specs=vmem(1)[0],
        compiler_params=pltpu.CompilerParams(vmem_limit_bytes=12 << 20),
        cost_estimate=pl.CostEstimate(
            flops=2 * slots * n * kv_width,
            bytes_accessed=6 * n * kv_width,
            transcendentals=0,
        ),
    )(picks, got_kv)

    def hop(x, up, down):
        return lax.ppermute(
            x,
            "ctx",
            [(c, (c + (2 * up if c % 2 == 0 else -2 * down)) % n_ctx) for c in range(n_ctx)],
        )

    def swap(x):
        return lax.ppermute(x, "ctx", [(c, c ^ 1) for c in range(n_ctx)])

    other = swap(own)
    pair = pl.pallas_call(
        join_kernel,
        out_shape=jax.ShapeDtypeStruct((2 * n, kv_width), keyvals.dtype),
        in_specs=vmem(2),
        out_specs=vmem(1)[0],
        compiler_params=pltpu.CompilerParams(vmem_limit_bytes=4 << 20),
        cost_estimate=pl.CostEstimate(
            flops=0, bytes_accessed=8 * n * kv_width, transcendentals=0
        ),
    )(own, other)
    hop1 = hop(pair, 1, 2)
    hop2 = hop(hop1, 1, 1)
    hop3 = hop(hop1, 2, 2)
    groups = width // head
    query = jax.ShapeDtypeStruct((n, 2 * width), queries.dtype)
    sums = jax.ShapeDtypeStruct((groups, head, n), jnp.float32)
    tops = jax.ShapeDtypeStruct((groups, 1, n), jnp.float32)
    totals = jax.ShapeDtypeStruct((groups, 8, n), jnp.float32)

    def attend(pieces, fresh, inputs, outputs, scratch, first=False, final=False):
        return pl.pallas_call(
            functools.partial(part_kernel, head, [f for f, _ in pieces], first, final),
            out_shape=outputs,
            in_specs=[pl.BlockSpec(memory_space=pltpu.SMEM)] + vmem(len(inputs) + len(pieces)),
            out_specs=pl.BlockSpec(memory_space=pl.ANY) if final else tuple(vmem(len(outputs))),
            scratch_shapes=[pltpu.VMEM((2 * n * fresh, kv_width), keyvals.dtype)] + scratch,
            compiler_params=pltpu.CompilerParams(vmem_limit_bytes=20 << 20),
            cost_estimate=pl.CostEstimate(
                flops=8 * n * n * width * fresh,
                bytes_accessed=8 * n * width,
                transcendentals=2 * n * n * groups * fresh,
            ),
        )(seq_lengths, *inputs, *[x for _, x in pieces])

    swapped1 = swap(hop1)
    early = [((0, 0), pair), ((1, 6), hop1), ((6, 1), swapped1)]
    swapped2 = swap(hop2)
    swapped3 = swap(hop3)
    middle = [((2, 5), hop2), ((5, 2), swapped2)]
    late = [((3, 4), hop3), ((4, 3), swapped3)]
    q_all, acc, top, total = attend(
        early, 3, (picks, got_q), (query, sums, tops, totals), [], first=True
    )
    acc, total = attend(middle, 2, (q_all, acc, top, total), (sums, totals), [])
    attended = attend(
        late + middle + early[::-1],
        2,
        (q_all, acc, top, total),
        jax.ShapeDtypeStruct((n, width), queries.dtype),
        [
            pltpu.VMEM(sums.shape, jnp.float32),
            pltpu.VMEM(tops.shape, jnp.float32),
            pltpu.VMEM(totals.shape, jnp.float32),
            pltpu.VMEM((n, width), queries.dtype),
            pltpu.SemaphoreType.DMA((groups,)),
        ],
        final=True,
    )
    return attended.reshape(1, n, width)


def solution(mesh):
    return jax.shard_map(
        body,
        mesh=mesh,
        in_specs=(
            P("dp", "ctx", None),
            P("dp", "ctx", None),
            P("dp", "ctx"),
            P("dp", "ctx"),
            P("dp", None),
        ),
        out_specs=P("dp", "ctx", None),
        check_vma=False,
    )
```

```python
import functools
import typing

import jax
import jax.numpy as jnp
from jax import lax
from jax.experimental import pallas as pl
from jax.experimental.pallas import tpu as pltpu
from jax.sharding import PartitionSpec as P


LOG2E = 1.4426950408889634
LOW = -1e30


def earlier_of(n):
    earlier = lax.broadcasted_iota(jnp.int32, (n, n), 0) < lax.broadcasted_iota(
        jnp.int32, (n, n), 1
    )
    return jnp.where(earlier, 1.0, 0.0).astype(jnp.bfloat16)


def slots_of(labels, earlier, owners, capacity):
    n = labels.shape[1]
    hot = lax.broadcasted_iota(jnp.int32, (owners, n), 0) == labels
    hot16 = jnp.where(hot, 1.0, 0.0).astype(jnp.bfloat16)
    before = jnp.dot(hot16, earlier, preferred_element_type=jnp.float32)
    rank = jnp.sum(jnp.where(hot, before, 0.0), axis=0, keepdims=True)
    return labels * capacity + rank.astype(jnp.int32)


def pack_kernel(owners, capacity, dest_hbm, rows_hbm, out_hbm, dest, rows, packed, sems):
    slots = owners * capacity
    n = rows.shape[0]
    fetch_dest = pltpu.make_async_copy(dest_hbm, dest, sems.at[0])
    fetch_rows = pltpu.make_async_copy(rows_hbm, rows, sems.at[1])
    fetch_dest.start()
    fetch_rows.start()
    earlier = earlier_of(n)
    fetch_dest.wait()
    slot = slots_of(dest[...], earlier, owners, capacity)
    half = slots // 2
    hot = [
        half * i + lax.broadcasted_iota(jnp.int32, (half, n), 0) == slot for i in range(2)
    ]
    picks = [jnp.where(h, 1.0, 0.0).astype(jnp.bfloat16) for h in hot]
    fetch_rows.wait()
    puts = []
    for i in range(2):
        part = pl.ds(half * i, half)
        packed[part, :] = jnp.dot(
            picks[i], rows[...], preferred_element_type=jnp.float32
        ).astype(packed.dtype)
        puts.append(
            pltpu.make_async_copy(packed.at[part, :], out_hbm.at[part, :], sems.at[2 + i])
        )
        puts[i].start()
    for put in puts:
        put.wait()


def picks_of(source_ref, owners, capacity):
    n = source_ref.shape[1]
    slots = slots_of(source_ref[...], earlier_of(n), owners, capacity)
    wide = jnp.broadcast_to(slots.astype(jnp.float32), (128, n))
    tall = jnp.transpose(wide).astype(jnp.int32)
    lane = lax.broadcasted_iota(jnp.int32, (n, 128), 1)
    parts = [
        jnp.where(tall == lane + 128 * i, 1.0, 0.0).astype(jnp.bfloat16)
        for i in range(owners * capacity // 128)
    ]
    return jnp.concatenate(parts, axis=1)


def picks_kernel(owners, capacity, source_ref, out_ref):
    out_ref[...] = picks_of(source_ref, owners, capacity)


def unpack_kernel(picks_ref, rows_ref, out_ref):
    out_ref[...] = jnp.dot(
        picks_ref[...], rows_ref[...], preferred_element_type=jnp.float32
    ).astype(out_ref.dtype)


def join_kernel(own_ref, other_ref, out_ref):
    n = own_ref.shape[0]
    core = lax.rem(lax.axis_index("ctx"), 2)
    out_ref[pl.ds(pl.multiple_of(core * n, n), n), :] = own_ref[...]
    out_ref[pl.ds(pl.multiple_of((1 - core) * n, n), n), :] = other_ref[...]


class Block(typing.NamedTuple):
    core: jax.Array
    own: jax.Array
    place: typing.Callable
    here: typing.Callable
    clear: typing.Callable
    late: typing.Callable
    step: typing.Callable


def block_of(head, far, lengths_ref, kv, q_all, acc, top, total):
    n = q_all.shape[0]
    groups = acc.shape[0]
    chunk = 2 * n
    me = lax.axis_index("ctx")
    chip = me // 2
    core = me - 2 * chip

    starts = [jnp.int32(0)]
    for i in range(lengths_ref.shape[1] - 1):
        starts.append(starts[-1] + lengths_ref[0, i])

    def start_of(position):
        found = jnp.zeros_like(position)
        for s in starts[1:]:
            found = jnp.where(position >= s, jnp.maximum(found, s), found)
        return found

    q_first = me * n
    q_pos = q_first + lax.broadcasted_iota(jnp.int32, (1, n), 1)
    q_start = start_of(q_pos)
    low = start_of(q_first)
    high = start_of(q_first + n - 1)

    def place(i):
        return (chip - jnp.where(core == 0, far[i][0], far[i][1])) * chunk

    def here(at):
        return (at >= 0) & (at + chunk > low)

    def clear(at):
        return (at >= high) & (at + chunk <= q_first)

    def late(at):
        return low >= at + n

    def tree_max(s):
        while s.shape[0] > 8:
            half = s.shape[0] // 2
            s = jnp.maximum(s[:half], s[half:])
        return jnp.max(s, axis=0, keepdims=True)

    def fold(w):
        return jnp.sum(w.reshape(-1, 8, w.shape[1]), axis=0)

    def step(row, rows, position, masked, mode):
        row = pl.multiple_of(row, n)
        keys = kv[pl.ds(row, rows), :head]
        values = jnp.transpose(kv[pl.ds(row, rows), head:])
        if masked:
            k_pos = position + lax.broadcasted_iota(jnp.int32, (rows, n), 0)
            visible = (k_pos <= q_pos) & (k_pos >= q_start)

        def scores(h):
            s = lax.dot_general(
                keys,
                q_all[:, h * head : (h + 1) * head],
                (((1,), (1,)), ((), ())),
                preferred_element_type=jnp.float32,
            ) * (LOG2E * head ** (-0.5))
            return jnp.where(visible, s, LOW) if masked else s

        def weigh(h, s):
            fade = None
            if mode == "fixed":
                m = top[h]
            elif mode == "first":
                m = tree_max(s)
                top[h] = m
            else:
                old = top[h]
                m = jnp.maximum(old, tree_max(s))
                top[h] = m
                fade = jnp.exp2(old - m)
            w = jnp.exp2(s - m)
            if mode == "fixed":
                total[h] += fold(w)
            elif mode == "first":
                total[h] = fold(w)
            else:
                total[h] = total[h] * fade + fold(w)
            return w.astype(kv.dtype), fade

        def gather(h, w, fade):
            part = jnp.dot(values, w, preferred_element_type=jnp.float32)
            if mode == "fixed":
                acc[h] += part
            elif mode == "first":
                acc[h] = part
            else:
                acc[h] = acc[h] * fade + part

        lag = 2
        s_of, w_of = {}, {}
        for t in range(groups + 1 + lag):
            if t < groups:
                s_of[t] = scores(t)
            if 0 <= t - 1 < groups:
                w_of[t - 1] = weigh(t - 1, s_of.pop(t - 1))
            if 0 <= t - 1 - lag < groups:
                gather(t - 1 - lag, *w_of.pop(t - 1 - lag))

    return Block(core, chip * chunk, place, here, clear, late, step)


def part_kernel(head, far, first, final, *refs):
    lengths_ref = refs[0]
    if first:
        picks_ref, got_ref = refs[1:3]
        near = refs[3 : 3 + len(far)]
        q_all, acc, top, total, kv = refs[3 + len(far) :]
        q_all[...] = jnp.dot(
            picks_ref[...], got_ref[...], preferred_element_type=jnp.float32
        ).astype(q_all.dtype)
    else:
        q_all, acc_ref, top_ref, total_ref = refs[1:5]
        near = refs[5 : 5 + len(far)]
        if final:
            out_ref, kv, acc, top, total, done, sems = refs[5 + len(far) :]
            top[...] = top_ref[...]
        else:
            acc, total, kv = refs[5 + len(far) :]
            top = top_ref
        acc[...] = acc_ref[...]
        total[...] = total_ref[...]
    n = q_all.shape[0]
    groups = acc.shape[0]
    chunk = 2 * n
    block = block_of(head, far, lengths_ref, kv, q_all, acc, top, total)

    def place(i, count):
        at = block.place(0)
        for j in range(1, count):
            at = jnp.where(i == j, block.place(j), at)
        return at

    skip = 1 if first else 0
    fresh = kv.shape[0] // chunk
    names = far[:fresh]
    for i in range(len(names)):

        @pl.when(block.here(block.place(i)))
        def _():
            kv[i * chunk : (i + 1) * chunk] = near[i][...]

    if first:

        @pl.when(block.core == 0)
        def _():
            block.step(0, n, block.own, True, "first")

        @pl.when(block.core != 0)
        def _():
            block.step(0, chunk, block.own, True, "first")

    @pl.loop(skip, len(names))
    def _(i):
        at = place(i, len(names))
        is_here = block.here(at)
        is_clear = block.clear(at)
        is_late = block.late(at)

        @pl.when(is_here & is_clear)
        def _():
            block.step(i * chunk, chunk, at, False, "fixed")

        @pl.when(is_here & jnp.logical_not(is_clear) & is_late)
        def _():
            block.step(i * chunk + n, n, at + n, True, "fixed")

        @pl.when(is_here & jnp.logical_not(is_clear | is_late))
        def _():
            block.step(i * chunk, chunk, at, True, "fixed")

    if not final:
        return

    most = total[0]
    for h in range(1, groups):
        most = jnp.maximum(most, total[h])

    @pl.when(jnp.max(most) > 2.0**64)
    def _():
        for h in range(groups):
            top[h] = jnp.full((1, n), LOW, jnp.float32)
            total[h] = jnp.zeros(total.shape[1:], jnp.float32)
            acc[h] = jnp.zeros(acc.shape[1:], jnp.float32)

        @pl.loop(0, len(far))
        def _(t):
            i = len(far) - 1 - t
            at = place(i, len(far))
            for j, ref in enumerate(near):

                @pl.when(i == j)
                def _():
                    kv[0:chunk] = ref[...]

            @pl.when(block.here(at))
            def _():
                block.step(0, chunk, at, True, "running")

    copies = []
    for h in range(groups):
        columns = pl.ds(h * head, head)
        share = 1.0 / jnp.sum(total[h], axis=0, keepdims=True)
        done[:, columns] = jnp.transpose((acc[h] * share).astype(done.dtype))
        copies.append(
            pltpu.make_async_copy(done.at[:, columns], out_ref.at[:, columns], sems.at[h])
        )
        copies[-1].start()
    for copy in copies:
        copy.wait()


def vmem(count):
    return [pl.BlockSpec(memory_space=pltpu.VMEM)] * count


def body(queries, keyvals, dest_bin, source_owner, seq_lengths):
    owners = lax.axis_size("dp")
    n_ctx = lax.axis_size("ctx")
    n = queries.shape[1]
    width = queries.shape[2]
    kv_width = keyvals.shape[2]
    head = kv_width // 2
    capacity = 2 * n // owners
    slots = owners * capacity

    def pack(rows):
        return pl.pallas_call(
            functools.partial(pack_kernel, owners, capacity),
            out_shape=jax.ShapeDtypeStruct((slots, rows.shape[1]), rows.dtype),
            in_specs=[pl.BlockSpec(memory_space=pl.ANY)] * 2,
            out_specs=pl.BlockSpec(memory_space=pl.ANY),
            scratch_shapes=[
                pltpu.VMEM(dest_bin.shape, dest_bin.dtype),
                pltpu.VMEM(rows.shape, rows.dtype),
                pltpu.VMEM((slots, rows.shape[1]), rows.dtype),
                pltpu.SemaphoreType.DMA((4,)),
            ],
            cost_estimate=pl.CostEstimate(
                flops=2 * slots * n * rows.shape[1],
                bytes_accessed=6 * n * rows.shape[1],
                transcendentals=0,
            ),
        )(dest_bin, rows)

    def exchange(rows):
        return lax.all_to_all(
            rows.reshape(owners, capacity, rows.shape[1]),
            "dp",
            split_axis=0,
            concat_axis=0,
            tiled=True,
        ).reshape(slots, rows.shape[1])

    got_kv = exchange(pack(keyvals[0]))
    got_q = exchange(pack(queries[0]))
    picks = pl.pallas_call(
        functools.partial(picks_kernel, owners, capacity),
        out_shape=jax.ShapeDtypeStruct((n, slots), keyvals.dtype),
        in_specs=vmem(1),
        out_specs=vmem(1)[0],
        compiler_params=pltpu.CompilerParams(vmem_limit_bytes=4 << 20),
        cost_estimate=pl.CostEstimate(
            flops=2 * n * n * owners, bytes_accessed=2 * n * slots, transcendentals=0
        ),
    )(source_owner)
    own = pl.pallas_call(
        unpack_kernel,
        out_shape=jax.ShapeDtypeStruct((n, kv_width), keyvals.dtype),
        in_specs=vmem(2),
        out_specs=vmem(1)[0],
        compiler_params=pltpu.CompilerParams(vmem_limit_bytes=12 << 20),
        cost_estimate=pl.CostEstimate(
            flops=2 * slots * n * kv_width,
            bytes_accessed=6 * n * kv_width,
            transcendentals=0,
        ),
    )(picks, got_kv)

    def hop(x, up, down):
        return lax.ppermute(
            x,
            "ctx",
            [(c, (c + (2 * up if c % 2 == 0 else -2 * down)) % n_ctx) for c in range(n_ctx)],
        )

    def swap(x):
        return lax.ppermute(x, "ctx", [(c, c ^ 1) for c in range(n_ctx)])

    other = swap(own)
    pair = pl.pallas_call(
        join_kernel,
        out_shape=jax.ShapeDtypeStruct((2 * n, kv_width), keyvals.dtype),
        in_specs=vmem(2),
        out_specs=vmem(1)[0],
        compiler_params=pltpu.CompilerParams(vmem_limit_bytes=4 << 20),
        cost_estimate=pl.CostEstimate(
            flops=0, bytes_accessed=8 * n * kv_width, transcendentals=0
        ),
    )(own, other)
    hop1 = hop(pair, 1, 2)
    hop2 = hop(hop1, 1, 1)
    hop3 = hop(hop1, 2, 2)
    groups = width // head
    query = jax.ShapeDtypeStruct((n, width), queries.dtype)
    sums = jax.ShapeDtypeStruct((groups, head, n), jnp.float32)
    tops = jax.ShapeDtypeStruct((groups, 1, n), jnp.float32)
    totals = jax.ShapeDtypeStruct((groups, 8, n), jnp.float32)

    def attend(pieces, fresh, inputs, outputs, scratch, first=False, final=False):
        return pl.pallas_call(
            functools.partial(part_kernel, head, [f for f, _ in pieces], first, final),
            out_shape=outputs,
            in_specs=[pl.BlockSpec(memory_space=pltpu.SMEM)] + vmem(len(inputs) + len(pieces)),
            out_specs=pl.BlockSpec(memory_space=pl.ANY) if final else tuple(vmem(len(outputs))),
            scratch_shapes=[pltpu.VMEM((2 * n * fresh, kv_width), keyvals.dtype)] + scratch,
            compiler_params=pltpu.CompilerParams(vmem_limit_bytes=20 << 20),
            cost_estimate=pl.CostEstimate(
                flops=8 * n * n * width * fresh,
                bytes_accessed=8 * n * width,
                transcendentals=2 * n * n * groups * fresh,
            ),
        )(seq_lengths, *inputs, *[x for _, x in pieces])

    swapped1 = swap(hop1)
    early = [((0, 0), pair), ((1, 6), hop1), ((6, 1), swapped1)]
    swapped2 = swap(hop2)
    swapped3 = swap(hop3)
    middle = [((3, 4), hop3), ((4, 3), swapped3)]
    late = [((2, 5), hop2), ((5, 2), swapped2)]
    q_all, acc, top, total = attend(
        early, 3, (picks, got_q), (query, sums, tops, totals), [], first=True
    )
    acc, total = attend(middle, 2, (q_all, acc, top, total), (sums, totals), [])
    attended = attend(
        late + middle + early[::-1],
        2,
        (q_all, acc, top, total),
        jax.ShapeDtypeStruct((n, width), queries.dtype),
        [
            pltpu.VMEM(sums.shape, jnp.float32),
            pltpu.VMEM(tops.shape, jnp.float32),
            pltpu.VMEM(totals.shape, jnp.float32),
            pltpu.VMEM((n, width), queries.dtype),
            pltpu.SemaphoreType.DMA((groups,)),
        ],
        final=True,
    )
    return attended.reshape(1, n, width)


def solution(mesh):
    return jax.shard_map(
        body,
        mesh=mesh,
        in_specs=(
            P("dp", "ctx", None),
            P("dp", "ctx", None),
            P("dp", "ctx"),
            P("dp", "ctx"),
            P("dp", None),
        ),
        out_specs=P("dp", "ctx", None),
        check_vma=False,
    )
```
